32 devices in a mesh: sub: 32 (over z, y, x, core).
Axes of the slice: x: 2, y: 2, z: 4, core: 2. Of those that a mesh axis runs over, the one named last changes fastest.
Arguments:
- images: float32 [2, 4, 512, 4096], P(None, None, 'sub'), may hold values from -6 to 6
- anchors: int32 [128], P('sub'), may hold values from 0 to 4095, as said below
- patches: int32 [128], P('sub'), may hold values from 0 to 31
- coeffs: float32 [4, 45, 32], P(None, None, 'sub'), may hold values from -1.2 to 1.2
- zbasis: float32 [45, 4096], replicated, may hold values from -4 to 4
Outputs:
- new_coeffs: float32 [4, 45, 32], P(None, None, 'sub')
- last_gradient: float32 [4, 45, 32], P(None, None, 'sub')
The draws below stay inside these ranges and needn't reach their ends.
Inputs may be any that keep to these rules, and one draw needn't show every extreme that they name: `anchors`: the first column of subfield s lies among the 128 columns that begin at 128 * (s // 4).
All inputs are finite; a program needn't handle non-finite values.
Results may differ from the reference program's by a relative error of at most 0.0003.
Values sent between devices are 32-bit elements; how exact they have to be, the bound alone decides.
A program may use at most 128 MiB of HBM per device.

```python
import math
import jax
import jax.numpy as jnp
import numpy as np
from jax import lax

SUB = 128
W = 4096
MODES = 45
CH = 2
FRAMES = 4
TR = 4
ITERS = 2
PUP = 64
H = 512
SUBS = 128
NP = 32


def draw_anchors(key, part):
    strip_width = W // (SUBS // TR)
    offsets = jax.random.randint(key, (SUBS,), 0, strip_width, dtype=jnp.int32)
    offsets = offsets.at[0].set(0).at[SUBS - 1].set(strip_width - 1)
    column_strips = jnp.arange(SUBS, dtype=jnp.int32) // TR
    return (column_strips * strip_width + offsets).astype(jnp.int32)


def set_ends(array, key, low, largest):
    longest = array.shape.index(max(array.shape))
    spots = []
    for shift in (0, 1):
        where = [jax.random.randint(jax.random.fold_in(key, axis), (), 0, length) for axis, length in enumerate(array.shape)]
        where[longest] = (where[longest] + shift) % array.shape[longest]
        spots.append(tuple(where))
    return array.at[spots[0]].set(low).at[spots[1]].set(largest)


def shard_levels(own_key, shape, shards, low, largest):
    level = 1.0
    for axis_at, parts in shards:
        steps = jax.random.uniform(jax.random.fold_in(jax.random.fold_in(own_key, 6), axis_at), (parts,), jnp.float32, low / len(shards), largest / len(shards))
        level = level * jnp.repeat(jnp.exp(steps), shape[axis_at] // parts).reshape((-1,) + (1,) * (len(shape) - 1 - axis_at))
    return level


def rank_bounds(number_of, lean):
    portions = [(1 << 20) // math.isqrt(rank ** lean) + 1 for rank in range(1, number_of + 1)]
    deviation = 1 + sum(portions) // (1 << 30)
    return np.cumsum(np.array([max(1, weight // deviation) for weight in portions]))


def ranked(own_key, dims, number_of, lean):
    grid = rank_bounds(number_of, lean)
    pick = jax.random.randint(jax.random.fold_in(own_key, 1), dims, 0, int(grid[number_of - 1]))
    grade = jnp.searchsorted(jnp.asarray(grid, jnp.int32), pick, side="right")
    return jax.random.permutation(jax.random.fold_in(own_key, 2), number_of)[grade].astype(jnp.int32)


def bell_draw(key, dims, spread, reach, shards=(), kind=jnp.bfloat16):
    result = spread * jax.random.normal(key, dims, jnp.float32)
    if shards:
        result = result * shard_levels(key, dims, shards, -0.22, 0.18)
    return jnp.clip(result, -reach, reach).astype(kind)


def setup_inputs(seed: int = 0) -> dict:
    keys = jax.random.split(jax.random.key(seed), 6)
    images = bell_draw(keys[0], (CH, FRAMES, H, W), 1.0, 6.0, ((2, 32),), jnp.float32)
    anchors = draw_anchors(jax.random.fold_in(keys[5], 71), 0)
    patches = set_ends(ranked(keys[2], (SUBS,), NP, 2), jax.random.fold_in(keys[2], 3), 0, NP - 1).astype(jnp.int32)
    coeffs = bell_draw(keys[3], (FRAMES, MODES, NP), 0.2, 1.2, ((2, 32),), jnp.float32)
    zbasis = bell_draw(keys[4], (MODES, PUP * PUP), 1.0, 4.0, (), jnp.float32)
    return {"images": images, "anchors": anchors, "patches": patches, "coeffs": coeffs, "zbasis": zbasis}


GAMMA = 0.01
STEP_SIZE = 0.05

def taper(length):
    cells = jnp.arange(length, dtype=jnp.float32)
    return 0.5 - 0.5 * jnp.cos(2.0 * math.pi * (cells + 0.5) / length)

def aperture(width):
    centred = jnp.arange(width, dtype=jnp.float32) - width / 2 + 0.5
    radius = centred[:, None] ** 2 + centred[None, :] ** 2
    return (radius <= (width / 2) ** 2).astype(jnp.float32)

def reference(images, anchors, patches, coeffs, zbasis):
    window_two = taper(SUB)[:, None] * taper(SUB)[None, :]
    padded = jnp.pad(images, ((0, 0), (0, 0), (0, 0), (0, SUB)))
    pupil_mask = aperture(PUP)
    pupil_area = jnp.sum(pupil_mask)
    ratios = 1.0 / (1.0 + 0.25 * jnp.arange(CH, dtype=jnp.float32))
    zero_index = jnp.zeros((), jnp.int32)

    def subfield_loss(coefficients, which):
        row_tile = (which % TR).astype(jnp.int32)
        start_row = (row_tile * SUB).astype(jnp.int32)
        start_col = anchors[which].astype(jnp.int32)
        window_cells = lax.dynamic_slice(padded, (zero_index, zero_index, start_row, start_col), (CH, FRAMES, SUB, SUB))
        spectrum = jnp.fft.fft2(window_cells * window_two)
        chosen = lax.dynamic_index_in_dim(coefficients, patches[which].astype(jnp.int32), axis=2, keepdims=False)
        phases = jnp.dot(chosen, zbasis, precision=lax.Precision.HIGHEST).reshape(FRAMES, PUP, PUP)
        scaled = ratios[:, None, None, None] * phases[None]
        pupil = pupil_mask * jnp.exp(1j * scaled)
        field = jnp.fft.fft2(pupil, s=(SUB, SUB))
        psf_values = jnp.abs(field) ** 2 / (SUB * SUB * pupil_area)
        otf = jnp.fft.fft2(psf_values)
        power_sum = lax.optimization_barrier(jnp.sum(jnp.abs(spectrum) ** 2, axis=1))
        cross = lax.optimization_barrier(jnp.sum(spectrum * jnp.conj(otf), axis=1))
        denominator = lax.optimization_barrier(jnp.sum(jnp.abs(otf) ** 2, axis=1)) + GAMMA
        return jnp.sum(power_sum - jnp.abs(cross) ** 2 / denominator) / SUB ** 4

    def total_loss(coefficients):
        losses = lax.map(lambda which: subfield_loss(coefficients, which), jnp.arange(SUBS, dtype=jnp.int32))
        return jnp.sum(losses)
    current = coeffs
    gradient = jnp.zeros_like(coeffs)
    for iteration in range(ITERS):
        gradient = jax.grad(total_loss)(current)
        current = current - STEP_SIZE * gradient
    return (current, gradient)
```

```python
import functools
import math

import jax
import jax.numpy as jnp
import ml_dtypes
import numpy as np
from jax import lax
from jax.experimental import pallas as pl
from jax.experimental.pallas import tpu as pltpu
from jax.sharding import PartitionSpec as P

SUB = 128
CH = 2
FRAMES = 4
TR = 4
ITERS = 2
PUP = 64
HALF = 72
GAMMA = 0.01
STEP_SIZE = 0.05
F32 = jnp.float32
BF16 = jnp.bfloat16
VMEM_LIMIT = 48 << 20
HIGHEST = lax.Precision.HIGHEST


def split_np(matrix):
    matrix = np.asarray(matrix, np.float32)
    high = matrix.astype(ml_dtypes.bfloat16)
    low = (matrix - high.astype(np.float32)).astype(ml_dtypes.bfloat16)
    return high, low


def make_tables():
    k = np.arange(SUB)
    angle = 2.0 * np.pi * (np.outer(k, k) % SUB) / SUB
    cos, sin = np.cos(angle), np.sin(angle)
    taper = 0.5 - 0.5 * np.cos(2.0 * np.pi * (k + 0.5) / SUB)
    right = np.zeros((2, 2, PUP, 2, 2, SUB))
    for half in range(2):
        right[0, half, :, half, 0] = cos[:PUP]
        right[0, half, :, half, 1] = -sin[:PUP]
        right[1, half, :, half, 0] = sin[:PUP]
        right[1, half, :, half, 1] = cos[:PUP]
    right = right.reshape(2 * SUB, 4 * SUB)
    left = np.block([[cos[:, :PUP], sin[:, :PUP]], [-sin[:, :PUP], cos[:, :PUP]]])
    rows_cos, rows_sin = np.zeros((HALF, SUB)), np.zeros((HALF, SUB))
    rows_cos[:65], rows_sin[:65] = cos[:65], sin[:65]
    rows = np.concatenate([rows_cos, rows_sin], 0)
    mixed = np.block([[cos, -sin], [-sin, -cos]])
    weight = np.zeros((HALF, 1))
    weight[:65] = 2.0
    weight[0] = weight[64] = 1.0
    centred = np.arange(PUP) - PUP / 2 + 0.5
    mask = (centred[:, None] ** 2 + centred[None, :] ** 2 <= (PUP / 2) ** 2).astype(np.float32)
    area = float(mask.sum())
    mask = mask.reshape(2, PUP // 2, PUP).transpose(1, 0, 2).reshape(PUP // 2, SUB)
    return {
        "right": right,
        "right_t": right.T,
        "left": left,
        "left_t": left.T,
        "rows": rows,
        "rows_t": rows.T,
        "mixed": mixed,
        "data_rows": rows * taper[None, :],
        "data_mixed": np.concatenate([taper, taper])[:, None] * mixed,
        "weight": np.broadcast_to(weight, (HALF, SUB)).astype(np.float32) * np.float32(-2.0 / SUB**4),
        "mask": np.tile(mask, (FRAMES, 1)),
        "area": area,
    }


def split(value):
    high = value.astype(BF16)
    low = (value - high.astype(F32)).astype(BF16)
    return high, low


def dot(a, b):
    return jnp.dot(a, b, preferred_element_type=F32)


def const_left(high_ref, low_ref, value):
    high, low = split(value)
    table = high_ref[...]
    return dot(table, high) + (dot(table, low) + dot(low_ref[...], high))


def const_right(value, high_ref, low_ref):
    high, low = split(value)
    table = high_ref[...]
    return dot(high, table) + (dot(low, table) + dot(high, low_ref[...]))


def sin_cos(angle):
    turns = jnp.floor(angle * np.float32(2.0 / math.pi) + 0.5)
    rest = angle - turns * np.float32(1.5703125)
    rest = rest - turns * np.float32(4.8351287841796875e-4)
    rest = rest - turns * np.float32(3.1385570764541626e-7)
    rest = rest - turns * np.float32(6.0771005065061922e-11)
    square = rest * rest
    sine = rest + rest * square * (
        -1.6666654611e-1 + square * (8.3321608736e-3 + square * -1.9515295891e-4)
    )
    cosine = 1.0 - 0.5 * square + square * square * (
        4.166664568298827e-2 + square * (-1.388731625493765e-3 + square * 2.443315711809948e-5)
    )
    quadrant = turns - 4.0 * jnp.floor(turns * 0.25)
    odd = (quadrant == 1.0) | (quadrant == 3.0)
    base_sin = jnp.where(odd, cosine, sine)
    base_cos = jnp.where(odd, sine, cosine)
    out_sin = jnp.where(quadrant >= 2.0, -base_sin, base_sin)
    out_cos = jnp.where((quadrant == 1.0) | (quadrant == 2.0), -base_cos, base_cos)
    return out_sin, out_cos


def half_plane(images, rows_high, rows_low, mixed_high, mixed_low):
    columns = const_left(rows_high, rows_low, images)
    stacked = jnp.concatenate(
        [
            jnp.concatenate(
                [columns[:HALF, f * SUB : (f + 1) * SUB], columns[HALF:, f * SUB : (f + 1) * SUB]], 1
            )
            for f in range(FRAMES)
        ],
        0,
    )
    return const_right(stacked, mixed_high, mixed_low)


def window_kernel(anchor_ref, image_ref, out_ref):
    anchor = anchor_ref[pl.program_id(0)]
    last = image_ref.shape[1] - SUB
    base = pl.multiple_of((anchor // SUB) * SUB, SUB)
    after = pl.multiple_of(jnp.minimum(base + SUB, last), SUB)
    shift = anchor - base
    first = image_ref[:, pl.ds(base, SUB)]
    second = image_ref[:, pl.ds(after, SUB)]
    second = jnp.where(base + SUB <= last, second, 0.0)
    both = jnp.concatenate([first, second], 1)
    out_ref[0] = pltpu.roll(both, 2 * SUB - shift, 1)[:, :SUB]


def data_kernel(cells_ref, rows_high, rows_low, mixed_high, mixed_low, out_ref):
    images = jnp.concatenate([cells_ref[0, f] for f in range(FRAMES)], 1)
    out_ref[0, 0] = half_plane(images, rows_high, rows_low, mixed_high, mixed_low)


def forward_kernel(
    scale,
    modes,
    coeff_ref,
    basis_ref,
    mask_ref,
    right_high,
    right_low,
    left_high,
    left_low,
    rows_high,
    rows_low,
    mixed_high,
    mixed_low,
    otf_ref,
    field_ref,
    pupil_ref,
):
    subfield = pl.program_id(0)
    channel = pl.program_id(1)
    ratio = 1.0 / (1.0 + 0.25 * channel.astype(F32))
    sums = [jnp.zeros((PUP // 2, SUB), F32) for _ in range(FRAMES)]
    for m in range(modes):
        mode = basis_ref[m]
        for f in range(FRAMES):
            sums[f] = sums[f] + coeff_ref[subfield * FRAMES + f, m] * mode
    phase = jnp.concatenate(sums, 0) * ratio
    sine, cosine = sin_cos(phase)
    mask = mask_ref[...]
    pupil = jnp.concatenate([mask * cosine, mask * sine], 1)
    pupil_ref[0, 0] = pupil
    half = const_right(pupil, right_high, right_low)
    q = PUP // 2
    blocks = jnp.concatenate(
        [
            jnp.concatenate(
                [half[f * q : (f + 1) * q, n * SUB : (n + 1) * SUB] for n in (0, 2, 1, 3)], 0
            )
            for f in range(FRAMES)
        ],
        1,
    )
    field = const_left(left_high, left_low, blocks)
    field_ref[0, 0] = field
    psf = (field[:SUB] * field[:SUB] + field[SUB:] * field[SUB:]) * scale
    otf_ref[0, 0] = half_plane(psf, rows_high, rows_low, mixed_high, mixed_low)


def backward_kernel(
    scale,
    data_ref,
    otf_ref,
    field_ref,
    pupil_ref,
    basis_ref,
    weight_ref,
    mixed_high,
    mixed_low,
    rows_high,
    rows_low,
    left_high,
    left_low,
    right_high,
    right_low,
    out_ref,
    phase_acc,
):
    channel = pl.program_id(1)
    ratio = 1.0 / (1.0 + 0.25 * channel.astype(F32))
    data = [data_ref[0, 0, f * HALF : (f + 1) * HALF, :] for f in range(FRAMES)]
    otf = [otf_ref[0, 0, f * HALF : (f + 1) * HALF, :] for f in range(FRAMES)]
    cross_real = cross_imag = power = None
    for f in range(FRAMES):
        dr, di = data[f][:, :SUB], data[f][:, SUB:]
        orr, oi = otf[f][:, :SUB], otf[f][:, SUB:]
        terms = (dr * orr + di * oi, di * orr - dr * oi, orr * orr + oi * oi)
        if f == 0:
            cross_real, cross_imag, power = terms
        else:
            cross_real = cross_real + terms[0]
            cross_imag = cross_imag + terms[1]
            power = power + terms[2]
    inverse = 1.0 / (power + GAMMA)
    slope = weight_ref[...] * inverse
    xr, xi = cross_real * inverse, cross_imag * inverse
    share = weight_ref[...] * (xr * xr + xi * xi)
    cross_real, cross_imag = cross_real * slope, cross_imag * slope
    bars = []
    for f in range(FRAMES):
        dr, di = data[f][:, :SUB], data[f][:, SUB:]
        orr, oi = otf[f][:, :SUB], otf[f][:, SUB:]
        bar_real = cross_real * dr + cross_imag * di - share * orr
        bar_imag = cross_real * di - cross_imag * dr - share * oi
        bars.append(jnp.concatenate([bar_real, bar_imag], 1))
    columns = const_right(jnp.concatenate(bars, 0), mixed_high, mixed_low)
    stacked = jnp.concatenate(
        [
            jnp.concatenate(
                [columns[f * HALF : (f + 1) * HALF, :SUB], columns[f * HALF : (f + 1) * HALF, SUB:]], 0
            )
            for f in range(FRAMES)
        ],
        1,
    )
    psf_bar = const_left(rows_high, rows_low, stacked) * (2.0 * scale)
    field = field_ref[0, 0]
    field_bar = jnp.concatenate([field[:SUB] * psf_bar, field[SUB:] * psf_bar], 0)
    half_bar = const_left(left_high, left_low, field_bar)
    q = PUP // 2
    rows = jnp.concatenate(
        [
            jnp.concatenate(
                [half_bar[n * q : (n + 1) * q, f * SUB : (f + 1) * SUB] for n in (0, 2, 1, 3)], 1
            )
            for f in range(FRAMES)
        ],
        0,
    )
    pupil_bar = const_right(rows, right_high, right_low)
    pupil = pupil_ref[0, 0]
    phase_bar = ratio * (pupil[:, :SUB] * pupil_bar[:, SUB:] - pupil[:, SUB:] * pupil_bar[:, :SUB])

    @pl.when(channel == 0)
    def _():
        phase_acc[...] = phase_bar

    @pl.when(channel == CH - 1)
    def _():
        total = phase_acc[...] + phase_bar
        modes = basis_ref.shape[0]
        ones = jnp.ones((8, SUB), F32)
        for f in range(FRAMES):
            part = jnp.sum(basis_ref[...] * total[f * q : (f + 1) * q][None], axis=1)
            line = lax.dot_general(
                ones, part, (((1,), (1,)), ((), ())), precision=HIGHEST, preferred_element_type=F32
            )
            out_ref[0, f : f + 1, :] = jnp.concatenate(
                [line[:1], jnp.zeros((1, SUB - modes), F32)], 1
            )


def gather_kernel(n, block_ref, out_ref, send_sem, recv_sem):
    me = lax.axis_index("sub")
    barrier = pltpu.get_barrier_semaphore()

    def greet(step, carry):
        pl.semaphore_signal(
            barrier,
            inc=1,
            device_id=(lax.rem(me + step, n),),
            device_id_type=pl.DeviceIdType.MESH,
        )
        return carry

    lax.fori_loop(1, n, greet, 0)
    pl.semaphore_wait(barrier, n - 1)

    def copy_to(step):
        return pltpu.make_async_remote_copy(
            src_ref=block_ref,
            dst_ref=out_ref.at[me],
            send_sem=send_sem.at[step],
            recv_sem=recv_sem.at[step],
            device_id=(lax.rem(me + step, n),),
            device_id_type=pl.DeviceIdType.MESH,
        )

    def begin(step, carry):
        copy_to(step).start()
        return carry

    def finish(step, carry):
        copy_to(step).wait()
        return carry

    lax.fori_loop(1, n, begin, 0)
    out_ref[me] = block_ref[...]
    lax.fori_loop(1, n, finish, 0)


def spread_blocks(block, ident):
    n = lax.axis_size("sub")
    return pl.pallas_call(
        functools.partial(gather_kernel, n),
        out_shape=jax.ShapeDtypeStruct((n,) + block.shape, F32),
        in_specs=[pl.BlockSpec(memory_space=pltpu.VMEM)],
        out_specs=pl.BlockSpec(memory_space=pltpu.VMEM),
        scratch_shapes=[pltpu.SemaphoreType.DMA((n,)), pltpu.SemaphoreType.DMA((n,))],
        compiler_params=pltpu.CompilerParams(collective_id=ident, has_side_effects=True),
    )(block)


def whole(array):
    return pl.BlockSpec(array.shape, lambda *_: (0,) * array.ndim, pipeline_mode=pl.Buffered(1))


def on_device(images, anchors, patches, coeffs, zbasis):
    devices = lax.axis_size("sub")
    device = lax.axis_index("sub")
    rows = images.shape[2]
    per = anchors.shape[0]
    owned = coeffs.shape[2]
    modes = coeffs.shape[1]
    tables = make_tables()
    pairs = {
        name: [jnp.asarray(part) for part in split_np(tables[name])]
        for name in tables
        if name not in ("weight", "mask", "area")
    }
    scale = float(1.0 / (SUB * SUB * tables["area"]))

    owned_rows = owned * FRAMES
    tile_rows = -(-(owned_rows + 2) // 8) * 8
    mine = jnp.zeros((tile_rows, SUB), F32)
    mine = mine.at[:owned_rows, :modes].set(coeffs.transpose(2, 0, 1).reshape(owned_rows, modes))
    mine = mine.at[owned_rows, :per].set(patches.astype(F32))
    mine = mine.at[owned_rows + 1, :per].set(anchors.astype(F32))
    everyone = spread_blocks(mine, 0)
    all_coeffs = everyone[:, :owned_rows, :].reshape(devices * owned, FRAMES * SUB)
    all_patches = everyone[:, owned_rows, :per].reshape(devices * per).astype(jnp.int32)
    tile = (device * rows) // SUB
    tile_anchors = lax.dynamic_index_in_dim(everyone[:, owned_rows + 1, :], tile, 1, keepdims=False)
    tile_anchors = tile_anchors.astype(jnp.int32)

    bands = images.reshape(CH * FRAMES * rows, images.shape[3])
    windows = pl.pallas_call(
        window_kernel,
        grid_spec=pltpu.PrefetchScalarGridSpec(
            num_scalar_prefetch=1,
            grid=(devices,),
            in_specs=[pl.BlockSpec(bands.shape, lambda j, a: (0, 0), pipeline_mode=pl.Buffered(1))],
            out_specs=pl.BlockSpec((1, bands.shape[0], SUB), lambda j, a: (j, 0, 0)),
        ),
        out_shape=jax.ShapeDtypeStruct((devices, bands.shape[0], SUB), F32),
        compiler_params=pltpu.CompilerParams(vmem_limit_bytes=VMEM_LIMIT),
    )(tile_anchors, bands)
    received = lax.all_to_all(windows, "sub", 0, 0, tiled=True)
    cells = received.reshape(TR, devices // TR, CH * FRAMES, rows, SUB)
    cells = cells.transpose(0, 2, 1, 3, 4).reshape(TR, CH * FRAMES, SUB, SUB)

    big = pltpu.CompilerParams(vmem_limit_bytes=VMEM_LIMIT)
    spectrum_shape = jax.ShapeDtypeStruct((per, CH, FRAMES * HALF, 2 * SUB), F32)

    def per_block(*tail):
        return pl.BlockSpec((1, 1) + tail, lambda s, c: (s, c, 0, 0))

    data_tables = pairs["data_rows"] + pairs["data_mixed"]
    data = pl.pallas_call(
        data_kernel,
        grid=(per, CH),
        in_specs=[pl.BlockSpec((1, FRAMES, SUB, SUB), lambda s, c: (s, c, 0, 0))]
        + [whole(t) for t in data_tables],
        out_specs=per_block(FRAMES * HALF, 2 * SUB),
        out_shape=spectrum_shape,
        compiler_params=big,
        cost_estimate=pl.CostEstimate(flops=6 * 10**9, bytes_accessed=5 << 20, transcendentals=0),
    )(cells, *data_tables)

    basis = zbasis.reshape(modes, 2, PUP // 2, PUP).transpose(0, 2, 1, 3).reshape(modes, PUP // 2, SUB)
    mask = jnp.asarray(tables["mask"])
    weight = jnp.asarray(tables["weight"])
    forward_tables = pairs["right"] + pairs["left"] + pairs["rows"] + pairs["mixed"]
    backward_tables = pairs["mixed"] + pairs["rows_t"] + pairs["left_t"] + pairs["right_t"]
    saved_shapes = [
        spectrum_shape,
        jax.ShapeDtypeStruct((per, CH, 2 * SUB, FRAMES * SUB), F32),
        jax.ShapeDtypeStruct((per, CH, FRAMES * PUP // 2, 2 * SUB), F32),
    ]
    saved_specs = [per_block(*s.shape[2:]) for s in saved_shapes]

    def slopes_of(chosen):
        flat = chosen.reshape(per * FRAMES, SUB)
        saved = pl.pallas_call(
            functools.partial(forward_kernel, scale, modes),
            grid=(per, CH),
            in_specs=[pl.BlockSpec(memory_space=pltpu.SMEM), whole(basis), whole(mask)]
            + [whole(t) for t in forward_tables],
            out_specs=saved_specs,
            out_shape=saved_shapes,
            compiler_params=big,
            cost_estimate=pl.CostEstimate(flops=10**10, bytes_accessed=8 << 20, transcendentals=0),
        )(flat, basis, mask, *forward_tables)
        return pl.pallas_call(
            functools.partial(backward_kernel, scale),
            grid=(per, CH),
            in_specs=[per_block(FRAMES * HALF, 2 * SUB)]
            + saved_specs
            + [whole(basis), whole(weight)]
            + [whole(t) for t in backward_tables],
            out_specs=pl.BlockSpec((1, FRAMES, SUB), lambda s, c: (s, 0, 0)),
            out_shape=jax.ShapeDtypeStruct((per, FRAMES, SUB), F32),
            scratch_shapes=[pltpu.VMEM((FRAMES * PUP // 2, SUB), F32)],
            compiler_params=big,
            cost_estimate=pl.CostEstimate(flops=10**10, bytes_accessed=8 << 20, transcendentals=0),
        )(data, *saved, basis, weight, *backward_tables)

    patch_ids = jnp.arange(devices * owned, dtype=jnp.int32)
    own_ids = device * owned + jnp.arange(owned, dtype=jnp.int32)
    wanted = jnp.concatenate([patches, own_ids])
    picks = (wanted[:, None] == patch_ids[None, :]).astype(F32)
    current = jnp.dot(picks, all_coeffs, precision=HIGHEST)
    sums = (wanted[:, None] == all_patches[None, :]).astype(F32)
    gradient = jnp.zeros_like(current)
    for iteration in range(ITERS):
        slopes = slopes_of(current[:per])
        gathered = spread_blocks(slopes.reshape(per * FRAMES, SUB), 1 + iteration)
        gathered = gathered.reshape(devices * per, FRAMES * SUB)
        gradient = jnp.dot(sums, gathered, precision=HIGHEST)
        current = current - STEP_SIZE * gradient

    def owned_part(value):
        return value[per:].reshape(owned, FRAMES, SUB)[:, :, :modes].transpose(1, 2, 0)

    return owned_part(current), owned_part(gradient)


def solution(mesh):
    return jax.shard_map(
        on_device,
        mesh=mesh,
        in_specs=(P(None, None, "sub", None), P("sub"), P("sub"), P(None, None, "sub"), P()),
        out_specs=(P(None, None, "sub"), P(None, None, "sub")),
        check_vma=False,
    )
```

```python
import functools
import math

import jax
import jax.numpy as jnp
import ml_dtypes
import numpy as np
from jax import lax
from jax.experimental import pallas as pl
from jax.experimental.pallas import tpu as pltpu
from jax.sharding import PartitionSpec as P

SUB = 128
CH = 2
FRAMES = 4
TR = 4
ITERS = 2
PUP = 64
HALF = 72
GAMMA = 0.01
STEP_SIZE = 0.05
F32 = jnp.float32
BF16 = jnp.bfloat16
VMEM_LIMIT = 48 << 20
HIGHEST = lax.Precision.HIGHEST


def split_np(matrix):
    matrix = np.asarray(matrix, np.float32)
    high = matrix.astype(ml_dtypes.bfloat16)
    low = (matrix - high.astype(np.float32)).astype(ml_dtypes.bfloat16)
    return high, low


def make_tables():
    k = np.arange(SUB)
    angle = 2.0 * np.pi * (np.outer(k, k) % SUB) / SUB
    cos, sin = np.cos(angle), np.sin(angle)
    taper = 0.5 - 0.5 * np.cos(2.0 * np.pi * (k + 0.5) / SUB)
    right = np.zeros((2, 2, PUP, 2, 2, SUB))
    for half in range(2):
        right[0, half, :, half, 0] = cos[:PUP]
        right[0, half, :, half, 1] = -sin[:PUP]
        right[1, half, :, half, 0] = sin[:PUP]
        right[1, half, :, half, 1] = cos[:PUP]
    right = right.reshape(2 * SUB, 4 * SUB)
    left = np.block([[cos[:, :PUP], sin[:, :PUP]], [-sin[:, :PUP], cos[:, :PUP]]])
    left = left.reshape(2 * SUB, 2, PUP // 2, 2).transpose(0, 1, 3, 2).reshape(2 * SUB, SUB)
    rows_cos, rows_sin = np.zeros((HALF, SUB)), np.zeros((HALF, SUB))
    rows_cos[:65], rows_sin[:65] = cos[:65], sin[:65]
    rows = np.concatenate([rows_cos, rows_sin], 0)
    mixed = np.block([[cos, -sin], [-sin, -cos]])
    weight = np.zeros((HALF, 1))
    weight[:65] = 2.0
    weight[0] = weight[64] = 1.0
    centred = np.arange(PUP) - PUP / 2 + 0.5
    mask = (centred[:, None] ** 2 + centred[None, :] ** 2 <= (PUP / 2) ** 2).astype(np.float32)
    area = float(mask.sum())
    mask = mask.reshape(PUP // 2, SUB)
    return {
        "right": right,
        "right_t": right.T,
        "left": left,
        "left_t": left.T,
        "rows": rows,
        "rows_t": rows.T,
        "mixed": mixed,
        "data_rows": rows * taper[None, :],
        "data_mixed": np.concatenate([taper, taper])[:, None] * mixed,
        "weight": np.broadcast_to(weight, (HALF, SUB)).astype(np.float32) * np.float32(-2.0 / SUB**4),
        "mask": np.tile(mask, (FRAMES, 1)),
        "area": area,
    }


def split(value):
    high = value.astype(BF16)
    low = (value - high.astype(F32)).astype(BF16)
    return high, low


def dot(a, b):
    return jnp.dot(a, b, preferred_element_type=F32)


def const_left(high_ref, low_ref, value):
    high, low = split(value)
    table = high_ref[...]
    return dot(table, high) + (dot(table, low) + dot(low_ref[...], high))


def const_right(value, high_ref, low_ref):
    high, low = split(value)
    table = high_ref[...]
    return dot(high, table) + (dot(low, table) + dot(high, low_ref[...]))


def sin_cos(angle):
    turns = jnp.floor(angle * np.float32(2.0 / math.pi) + 0.5)
    rest = angle - turns * np.float32(1.5703125)
    rest = rest - turns * np.float32(4.8351287841796875e-4)
    rest = rest - turns * np.float32(3.1385570764541626e-7)
    rest = rest - turns * np.float32(6.0771005065061922e-11)
    square = rest * rest
    sine = rest + rest * square * (
        -1.6666654611e-1 + square * (8.3321608736e-3 + square * -1.9515295891e-4)
    )
    cosine = 1.0 - 0.5 * square + square * square * (
        4.166664568298827e-2 + square * (-1.388731625493765e-3 + square * 2.443315711809948e-5)
    )
    quadrant = turns - 4.0 * jnp.floor(turns * 0.25)
    odd = (quadrant == 1.0) | (quadrant == 3.0)
    base_sin = jnp.where(odd, cosine, sine)
    base_cos = jnp.where(odd, sine, cosine)
    out_sin = jnp.where(quadrant >= 2.0, -base_sin, base_sin)
    out_cos = jnp.where((quadrant == 1.0) | (quadrant == 2.0), -base_cos, base_cos)
    return out_sin, out_cos


def half_plane(images, rows_high, rows_low, mixed_high, mixed_low):
    columns = const_left(rows_high, rows_low, images)
    stacked = jnp.concatenate(
        [
            jnp.concatenate(
                [columns[:HALF, f * SUB : (f + 1) * SUB], columns[HALF:, f * SUB : (f + 1) * SUB]], 1
            )
            for f in range(FRAMES)
        ],
        0,
    )
    return const_right(stacked, mixed_high, mixed_low)


def window_kernel(batch, anchor_ref, image_ref, out_ref):
    last = image_ref.shape[1] - SUB
    lane = lax.broadcasted_iota(jnp.int32, (image_ref.shape[0], SUB), 1)
    for k in range(batch):
        anchor = anchor_ref[pl.program_id(0) * batch + k]
        base = pl.multiple_of((anchor // SUB) * SUB, SUB)
        after = pl.multiple_of(jnp.minimum(base + SUB, last), SUB)
        shift = anchor - base
        turn = lax.rem(SUB - shift, SUB)
        first = pltpu.roll(image_ref[:, pl.ds(base, SUB)], turn, 1)
        second = pltpu.roll(image_ref[:, pl.ds(after, SUB)], turn, 1)
        reach = jnp.where(base + SUB <= last, SUB, 0)
        out_ref[k] = jnp.where(
            lane < SUB - shift, first, jnp.where(lane < reach, second, 0.0)
        )


def data_kernel(cells_ref, rows_high, rows_low, mixed_high, mixed_low, out_ref):
    images = jnp.concatenate([cells_ref[:, 0, 0, f].reshape(SUB, SUB) for f in range(FRAMES)], 1)
    out_ref[0, 0] = half_plane(images, rows_high, rows_low, mixed_high, mixed_low)


def forward_kernel(
    scale,
    modes,
    coeff_ref,
    basis_ref,
    mask_ref,
    right_high,
    right_low,
    left_high,
    left_low,
    rows_high,
    rows_low,
    mixed_high,
    mixed_low,
    otf_ref,
    field_ref,
    pupil_ref,
):
    subfield = pl.program_id(0)
    channel = pl.program_id(1)
    ratio = 1.0 / (1.0 + 0.25 * channel.astype(F32))
    sums = [jnp.zeros((PUP // 2, SUB), F32) for _ in range(FRAMES)]
    for m in range(modes):
        mode = basis_ref[m]
        for f in range(FRAMES):
            sums[f] = sums[f] + coeff_ref[subfield * FRAMES + f, m] * mode
    phase = jnp.concatenate(sums, 0) * ratio
    sine, cosine = sin_cos(phase)
    mask = mask_ref[...]
    pupil = jnp.concatenate([mask * cosine, mask * sine], 1)
    pupil_ref[0, 0] = pupil
    half = const_right(pupil, right_high, right_low)
    q = PUP // 2
    blocks = jnp.concatenate(
        [
            jnp.concatenate(
                [half[f * q : (f + 1) * q, n * SUB : (n + 1) * SUB] for n in (0, 2, 1, 3)], 0
            )
            for f in range(FRAMES)
        ],
        1,
    )
    field = const_left(left_high, left_low, blocks)
    field_ref[0, 0] = field
    psf = (field[:SUB] * field[:SUB] + field[SUB:] * field[SUB:]) * scale
    otf_ref[0, 0] = half_plane(psf, rows_high, rows_low, mixed_high, mixed_low)


def backward_kernel(
    scale,
    data_ref,
    otf_ref,
    field_ref,
    pupil_ref,
    basis_ref,
    weight_ref,
    mixed_high,
    mixed_low,
    rows_high,
    rows_low,
    left_high,
    left_low,
    right_high,
    right_low,
    out_ref,
    phase_acc,
):
    channel = pl.program_id(1)
    ratio = 1.0 / (1.0 + 0.25 * channel.astype(F32))
    data = [data_ref[0, 0, f * HALF : (f + 1) * HALF, :] for f in range(FRAMES)]
    otf = [otf_ref[0, 0, f * HALF : (f + 1) * HALF, :] for f in range(FRAMES)]
    cross_real = cross_imag = power = None
    for f in range(FRAMES):
        dr, di = data[f][:, :SUB], data[f][:, SUB:]
        orr, oi = otf[f][:, :SUB], otf[f][:, SUB:]
        terms = (dr * orr + di * oi, di * orr - dr * oi, orr * orr + oi * oi)
        if f == 0:
            cross_real, cross_imag, power = terms
        else:
            cross_real = cross_real + terms[0]
            cross_imag = cross_imag + terms[1]
            power = power + terms[2]
    inverse = 1.0 / (power + GAMMA)
    slope = weight_ref[...] * inverse
    xr, xi = cross_real * inverse, cross_imag * inverse
    share = weight_ref[...] * (xr * xr + xi * xi)
    cross_real, cross_imag = cross_real * slope, cross_imag * slope
    bars = []
    for f in range(FRAMES):
        dr, di = data[f][:, :SUB], data[f][:, SUB:]
        orr, oi = otf[f][:, :SUB], otf[f][:, SUB:]
        bar_real = cross_real * dr + cross_imag * di - share * orr
        bar_imag = cross_real * di - cross_imag * dr - share * oi
        bars.append(jnp.concatenate([bar_real, bar_imag], 1))
    columns = const_right(jnp.concatenate(bars, 0), mixed_high, mixed_low)
    stacked = jnp.concatenate(
        [
            jnp.concatenate(
                [columns[f * HALF : (f + 1) * HALF, :SUB], columns[f * HALF : (f + 1) * HALF, SUB:]], 0
            )
            for f in range(FRAMES)
        ],
        1,
    )
    psf_bar = const_left(rows_high, rows_low, stacked) * (2.0 * scale)
    field = field_ref[0, 0]
    field_bar = jnp.concatenate([field[:SUB] * psf_bar, field[SUB:] * psf_bar], 0)
    half_bar = const_left(left_high, left_low, field_bar)
    q = PUP // 2
    rows = jnp.concatenate(
        [
            jnp.concatenate(
                [half_bar[n * q : (n + 1) * q, f * SUB : (f + 1) * SUB] for n in (0, 2, 1, 3)], 1
            )
            for f in range(FRAMES)
        ],
        0,
    )
    pupil_bar = const_right(rows, right_high, right_low)
    pupil = pupil_ref[0, 0]
    phase_bar = ratio * (pupil[:, :SUB] * pupil_bar[:, SUB:] - pupil[:, SUB:] * pupil_bar[:, :SUB])

    @pl.when(channel == 0)
    def _():
        phase_acc[...] = phase_bar

    @pl.when(channel == CH - 1)
    def _():
        total = phase_acc[...] + phase_bar
        modes = basis_ref.shape[0]
        ones = jnp.ones((8, SUB), F32)
        for f in range(FRAMES):
            part = jnp.sum(basis_ref[...] * total[f * q : (f + 1) * q][None], axis=1)
            line = lax.dot_general(
                ones, part, (((1,), (1,)), ((), ())), precision=HIGHEST, preferred_element_type=F32
            )
            out_ref[0, f : f + 1, :] = jnp.concatenate(
                [line[:1], jnp.zeros((1, SUB - modes), F32)], 1
            )


def gather_kernel(n, block_ref, out_ref, send_sem, recv_sem):
    me = lax.axis_index("sub")
    barrier = pltpu.get_barrier_semaphore()

    def greet(step, carry):
        pl.semaphore_signal(
            barrier,
            inc=1,
            device_id=(lax.rem(me + step, n),),
            device_id_type=pl.DeviceIdType.MESH,
        )
        return carry

    lax.fori_loop(1, n, greet, 0)
    pl.semaphore_wait(barrier, n - 1)

    def copy_to(step):
        return pltpu.make_async_remote_copy(
            src_ref=block_ref,
            dst_ref=out_ref.at[me],
            send_sem=send_sem.at[step],
            recv_sem=recv_sem.at[step],
            device_id=(lax.rem(me + step, n),),
            device_id_type=pl.DeviceIdType.MESH,
        )

    def begin(step, carry):
        copy_to(step).start()
        return carry

    def finish(step, carry):
        copy_to(step).wait()
        return carry

    lax.fori_loop(1, n, begin, 0)
    out_ref[me] = block_ref[...]
    lax.fori_loop(1, n, finish, 0)


def spread_blocks(block, ident):
    n = lax.axis_size("sub")
    return pl.pallas_call(
        functools.partial(gather_kernel, n),
        out_shape=jax.ShapeDtypeStruct((n,) + block.shape, F32),
        in_specs=[pl.BlockSpec(memory_space=pltpu.VMEM)],
        out_specs=pl.BlockSpec(memory_space=pltpu.VMEM),
        scratch_shapes=[pltpu.SemaphoreType.DMA((n,)), pltpu.SemaphoreType.DMA((n,))],
        compiler_params=pltpu.CompilerParams(collective_id=ident, has_side_effects=True),
    )(block)


def whole(array):
    return pl.BlockSpec(array.shape, lambda *_: (0,) * array.ndim, pipeline_mode=pl.Buffered(1))


def on_device(images, anchors, patches, coeffs, zbasis):
    devices = lax.axis_size("sub")
    device = lax.axis_index("sub")
    rows = images.shape[2]
    per = anchors.shape[0]
    owned = coeffs.shape[2]
    modes = coeffs.shape[1]
    tables = make_tables()
    pairs = {
        name: [jnp.asarray(part) for part in split_np(tables[name])]
        for name in tables
        if name not in ("weight", "mask", "area")
    }
    scale = float(1.0 / (SUB * SUB * tables["area"]))

    owned_rows = owned * FRAMES
    tile_rows = -(-(owned_rows + 2) // 8) * 8
    mine = jnp.zeros((tile_rows, SUB), F32)
    mine = mine.at[:owned_rows, :modes].set(coeffs.transpose(2, 0, 1).reshape(owned_rows, modes))
    owned_row_patch = owned_rows
    mine = mine.at[owned_rows, :per].set(patches.astype(F32))
    mine = mine.at[owned_rows + 1, :per].set(anchors.astype(F32))
    everyone = spread_blocks(mine, 0)
    all_coeffs = everyone[:, :owned_rows, :].reshape(devices * owned, FRAMES * SUB)
    group = devices // TR
    tile = device // group
    place = device % group
    share = devices * per // TR // group
    all_patches = everyone[:, owned_row_patch, :per].reshape(devices * per // TR, TR)
    all_anchors = everyone[:, owned_row_patch + 1, :per].reshape(devices * per // TR, TR)
    all_patches = all_patches.astype(jnp.int32).T
    pick_tile = (jnp.arange(TR, dtype=jnp.int32) == tile)[None, :]
    tile_anchors = jnp.sum(jnp.where(pick_tile, all_anchors, 0.0), axis=1).astype(jnp.int32)
    patches = lax.dynamic_slice(all_patches, (tile, place * share), (1, share)).reshape(share)
    all_patches = all_patches.reshape(devices * per)

    count = devices * per // TR
    batch = 8
    bands = images.reshape(CH * FRAMES * rows, images.shape[3])
    windows = pl.pallas_call(
        functools.partial(window_kernel, batch),
        grid_spec=pltpu.PrefetchScalarGridSpec(
            num_scalar_prefetch=1,
            grid=(count // batch,),
            in_specs=[pl.BlockSpec(bands.shape, lambda j, a: (0, 0), pipeline_mode=pl.Buffered(1))],
            out_specs=pl.BlockSpec((batch, bands.shape[0], SUB), lambda j, a: (j, 0, 0)),
        ),
        out_shape=jax.ShapeDtypeStruct((count, bands.shape[0], SUB), F32),
        compiler_params=pltpu.CompilerParams(vmem_limit_bytes=VMEM_LIMIT),
    )(tile_anchors, bands)
    teams = [list(range(g * group, (g + 1) * group)) for g in range(TR)]
    received = lax.all_to_all(windows, "sub", 0, 0, axis_index_groups=teams, tiled=True)
    cells = received.reshape(group, share, CH, FRAMES, rows, SUB)
    if rows % 8:
        cells = cells.transpose(1, 2, 3, 0, 4, 5).reshape(1, share, CH, FRAMES, SUB, SUB)
    per = share

    big = pltpu.CompilerParams(vmem_limit_bytes=VMEM_LIMIT)
    spectrum_shape = jax.ShapeDtypeStruct((per, CH, FRAMES * HALF, 2 * SUB), F32)

    def per_block(*tail):
        return pl.BlockSpec((1, 1) + tail, lambda s, c: (s, c, 0, 0))

    data_tables = pairs["data_rows"] + pairs["data_mixed"]
    data = pl.pallas_call(
        data_kernel,
        grid=(per, CH),
        in_specs=[
            pl.BlockSpec(
                (cells.shape[0], 1, 1) + cells.shape[3:], lambda s, c: (0, s, c, 0, 0, 0)
            )
        ]
        + [whole(t) for t in data_tables],
        out_specs=per_block(FRAMES * HALF, 2 * SUB),
        out_shape=spectrum_shape,
        compiler_params=big,
        cost_estimate=pl.CostEstimate(flops=6 * 10**9, bytes_accessed=5 << 20, transcendentals=0),
    )(cells, *data_tables)

    basis = zbasis.reshape(modes, PUP // 2, SUB)
    mask = jnp.asarray(tables["mask"])
    weight = jnp.asarray(tables["weight"])
    forward_tables = pairs["right"] + pairs["left"] + pairs["rows"] + pairs["mixed"]
    backward_tables = pairs["mixed"] + pairs["rows_t"] + pairs["left_t"] + pairs["right_t"]
    saved_shapes = [
        spectrum_shape,
        jax.ShapeDtypeStruct((per, CH, 2 * SUB, FRAMES * SUB), F32),
        jax.ShapeDtypeStruct((per, CH, FRAMES * PUP // 2, 2 * SUB), F32),
    ]
    saved_specs = [per_block(*s.shape[2:]) for s in saved_shapes]

    def slopes_of(chosen):
        flat = chosen.reshape(per * FRAMES, SUB)
        saved = pl.pallas_call(
            functools.partial(forward_kernel, scale, modes),
            grid=(per, CH),
            in_specs=[pl.BlockSpec(memory_space=pltpu.SMEM), whole(basis), whole(mask)]
            + [whole(t) for t in forward_tables],
            out_specs=saved_specs,
            out_shape=saved_shapes,
            compiler_params=big,
            cost_estimate=pl.CostEstimate(flops=10**10, bytes_accessed=8 << 20, transcendentals=0),
        )(flat, basis, mask, *forward_tables)
        return pl.pallas_call(
            functools.partial(backward_kernel, scale),
            grid=(per, CH),
            in_specs=[per_block(FRAMES * HALF, 2 * SUB)]
            + saved_specs
            + [whole(basis), whole(weight)]
            + [whole(t) for t in backward_tables],
            out_specs=pl.BlockSpec((1, FRAMES, SUB), lambda s, c: (s, 0, 0)),
            out_shape=jax.ShapeDtypeStruct((per, FRAMES, SUB), F32),
            scratch_shapes=[pltpu.VMEM((FRAMES * PUP // 2, SUB), F32)],
            compiler_params=big,
            cost_estimate=pl.CostEstimate(flops=10**10, bytes_accessed=8 << 20, transcendentals=0),
        )(data, *saved, basis, weight, *backward_tables)

    patch_ids = jnp.arange(devices * owned, dtype=jnp.int32)
    own_ids = device * owned + jnp.arange(owned, dtype=jnp.int32)
    wanted = jnp.concatenate([patches, own_ids])
    picks = (wanted[:, None] == patch_ids[None, :]).astype(F32)
    current = jnp.dot(picks, all_coeffs, precision=HIGHEST)
    sums = (wanted[:, None] == all_patches[None, :]).astype(F32)
    gradient = jnp.zeros_like(current)
    for iteration in range(ITERS):
        slopes = slopes_of(current[:per])
        gathered = spread_blocks(slopes.reshape(per * FRAMES, SUB), 1 + iteration)
        gathered = gathered.reshape(devices * per, FRAMES * SUB)
        gradient = jnp.dot(sums, gathered, precision=HIGHEST)
        current = current - STEP_SIZE * gradient

    def owned_part(value):
        return value[per:].reshape(owned, FRAMES, SUB)[:, :, :modes].transpose(1, 2, 0)

    return owned_part(current), owned_part(gradient)


def solution(mesh):
    return jax.shard_map(
        on_device,
        mesh=mesh,
        in_specs=(P(None, None, "sub", None), P("sub"), P("sub"), P(None, None, "sub"), P()),
        out_specs=(P(None, None, "sub"), P(None, None, "sub")),
        check_vma=False,
    )
```

```python
import functools
import math

import jax
import jax.numpy as jnp
import ml_dtypes
import numpy as np
from jax import lax
from jax.experimental import pallas as pl
from jax.experimental.pallas import tpu as pltpu
from jax.sharding import PartitionSpec as P

SUB = 128
CH = 2
FRAMES = 4
FIELDS = CH * FRAMES
SLOT = 64
TR = 4
ITERS = 2
PUP = 64
HALF = 72
GAMMA = 0.01
STEP_SIZE = 0.05
F32 = jnp.float32
BF16 = jnp.bfloat16
VMEM_LIMIT = 48 << 20
HIGHEST = lax.Precision.HIGHEST


def split_np(matrix):
    matrix = np.asarray(matrix, np.float32)
    high = matrix.astype(ml_dtypes.bfloat16)
    low = (matrix - high.astype(np.float32)).astype(ml_dtypes.bfloat16)
    return high, low


def make_tables():
    k = np.arange(SUB)
    angle = 2.0 * np.pi * (np.outer(k, k) % SUB) / SUB
    cos, sin = np.cos(angle), np.sin(angle)
    taper = 0.5 - 0.5 * np.cos(2.0 * np.pi * (k + 0.5) / SUB)
    right = np.zeros((2, 2, PUP, 2, 2, SUB))
    for half in range(2):
        right[0, half, :, half, 0] = cos[:PUP]
        right[0, half, :, half, 1] = -sin[:PUP]
        right[1, half, :, half, 0] = sin[:PUP]
        right[1, half, :, half, 1] = cos[:PUP]
    right = right.reshape(2 * SUB, 4 * SUB)
    left = np.block([[cos[:, :PUP], sin[:, :PUP]], [-sin[:, :PUP], cos[:, :PUP]]])
    left = left.reshape(2 * SUB, 2, PUP // 2, 2).transpose(0, 1, 3, 2).reshape(2 * SUB, SUB)
    rows_cos, rows_sin = np.zeros((HALF, SUB)), np.zeros((HALF, SUB))
    rows_cos[:65], rows_sin[:65] = cos[:65], sin[:65]
    rows = np.concatenate([rows_cos, rows_sin], 0)
    mixed = np.block([[cos, -sin], [-sin, -cos]])
    weight = np.zeros((HALF, 1))
    weight[:65] = 2.0
    weight[0] = weight[64] = 1.0
    centred = np.arange(PUP) - PUP / 2 + 0.5
    mask = (centred[:, None] ** 2 + centred[None, :] ** 2 <= (PUP / 2) ** 2).astype(np.float32)
    area = float(mask.sum())
    mask = mask.reshape(PUP // 2, SUB)
    return {
        "right": right,
        "right_t": right.T,
        "left": left,
        "left_t": left.T,
        "rows": rows,
        "rows_t": rows.T,
        "mixed": mixed,
        "data_rows": rows * taper[None, :],
        "data_mixed": np.concatenate([taper, taper])[:, None] * mixed,
        "weight": np.broadcast_to(weight, (HALF, SUB)).astype(np.float32) * np.float32(-2.0 / SUB**4),
        "mask": np.tile(mask, (FIELDS, 1)),
        "area": area,
    }


def split(value):
    high = value.astype(BF16)
    low = (value - high.astype(F32)).astype(BF16)
    return high, low


def dot(a, b):
    return jnp.dot(a, b, preferred_element_type=F32)


def const_left(high_ref, low_ref, value):
    high, low = split(value)
    table = high_ref[...]
    return dot(table, high) + (dot(table, low) + dot(low_ref[...], high))


def const_right(value, high_ref, low_ref):
    high, low = split(value)
    table = high_ref[...]
    return dot(high, table) + (dot(low, table) + dot(high, low_ref[...]))


def sin_cos(angle):
    turns = jnp.floor(angle * np.float32(2.0 / math.pi) + 0.5)
    rest = angle - turns * np.float32(1.5703125)
    rest = rest - turns * np.float32(4.8351287841796875e-4)
    rest = rest - turns * np.float32(3.1385570764541626e-7)
    rest = rest - turns * np.float32(6.0771005065061922e-11)
    square = rest * rest
    sine = rest + rest * square * (
        -1.6666654611e-1 + square * (8.3321608736e-3 + square * -1.9515295891e-4)
    )
    cosine = 1.0 - 0.5 * square + square * square * (
        4.166664568298827e-2 + square * (-1.388731625493765e-3 + square * 2.443315711809948e-5)
    )
    quadrant = turns - 4.0 * jnp.floor(turns * 0.25)
    odd = (quadrant == 1.0) | (quadrant == 3.0)
    base_sin = jnp.where(odd, cosine, sine)
    base_cos = jnp.where(odd, sine, cosine)
    out_sin = jnp.where(quadrant >= 2.0, -base_sin, base_sin)
    out_cos = jnp.where((quadrant == 1.0) | (quadrant == 2.0), -base_cos, base_cos)
    return out_sin, out_cos


def stacked_left(twice_ref, low_ref, value):
    high, low = split(value)
    return dot(twice_ref[...], jnp.concatenate([high, low], 0)) + dot(low_ref[...], high)


def half_plane(images, rows_twice, rows_low, mixed_high, mixed_low):
    columns = stacked_left(rows_twice, rows_low, images)
    stacked = jnp.concatenate(
        [
            jnp.concatenate(
                [columns[:HALF, f * SUB : (f + 1) * SUB], columns[HALF:, f * SUB : (f + 1) * SUB]], 1
            )
            for f in range(FIELDS)
        ],
        0,
    )
    return const_right(stacked, mixed_high, mixed_low)


def window_kernel(batch, anchor_ref, image_ref, out_ref):
    last = image_ref.shape[1] - SUB
    lane = lax.broadcasted_iota(jnp.int32, (image_ref.shape[0], SUB), 1)
    for k in range(batch):
        anchor = anchor_ref[pl.program_id(0) * batch + k]
        base = pl.multiple_of((anchor // SUB) * SUB, SUB)
        after = pl.multiple_of(jnp.minimum(base + SUB, last), SUB)
        shift = anchor - base
        turn = lax.rem(SUB - shift, SUB)
        first = pltpu.roll(image_ref[:, pl.ds(base, SUB)], turn, 1)
        second = pltpu.roll(image_ref[:, pl.ds(after, SUB)], turn, 1)
        reach = jnp.where(base + SUB <= last, SUB, 0)
        out_ref[k] = jnp.where(
            lane < SUB - shift, first, jnp.where(lane < reach, second, 0.0)
        )


def forward_math(scale, modes, coeff_ref, basis_ref, mask_ref, tables):
    right_high, right_low, left_twice, left_low, rows_twice, rows_low, mixed_high, mixed_low = tables
    subfield = pl.program_id(0)
    q = PUP // 2
    sums = [jnp.zeros((q, SUB), F32) for _ in range(FRAMES)]
    for m in range(modes):
        mode = basis_ref[m]
        for f in range(FRAMES):
            value = coeff_ref[subfield * 2 + f // 2, (f % 2) * SLOT + m]
            sums[f] = sums[f] + value * mode
    phase = jnp.concatenate(sums, 0)
    phase = jnp.concatenate([phase * np.float32(1.0 / (1.0 + 0.25 * c)) for c in range(CH)], 0)
    sine, cosine = sin_cos(phase)
    mask = mask_ref[...]
    pupil = jnp.concatenate([mask * cosine, mask * sine], 1)
    half = const_right(pupil, right_high, right_low)
    blocks = jnp.concatenate(
        [
            jnp.concatenate(
                [half[f * q : (f + 1) * q, n * SUB : (n + 1) * SUB] for n in (0, 2, 1, 3)], 0
            )
            for f in range(FIELDS)
        ],
        1,
    )
    field = stacked_left(left_twice, left_low, blocks)
    psf = (field[:SUB] * field[:SUB] + field[SUB:] * field[SUB:]) * scale
    return half_plane(psf, rows_twice, rows_low, mixed_high, mixed_low), field, pupil


def backward_math(scale, data, otf, field, pupil, basis_ref, weight_ref, tables):
    mixed_high, mixed_low, rows_high, rows_low, left_high, left_low, right_high, right_low = tables
    weight = weight_ref[...]
    bars = []
    for c in range(CH):
        parts = []
        cross_real = cross_imag = power = None
        for f in range(c * FRAMES, (c + 1) * FRAMES):
            d, o = data[f * HALF : (f + 1) * HALF], otf[f * HALF : (f + 1) * HALF]
            dr, di, orr, oi = d[:, :SUB], d[:, SUB:], o[:, :SUB], o[:, SUB:]
            parts.append((dr, di, orr, oi))
            terms = (dr * orr + di * oi, di * orr - dr * oi, orr * orr + oi * oi)
            if cross_real is None:
                cross_real, cross_imag, power = terms
            else:
                cross_real = cross_real + terms[0]
                cross_imag = cross_imag + terms[1]
                power = power + terms[2]
        inverse = 1.0 / (power + GAMMA)
        slope = weight * inverse
        xr, xi = cross_real * inverse, cross_imag * inverse
        share = weight * (xr * xr + xi * xi)
        cross_real, cross_imag = cross_real * slope, cross_imag * slope
        for dr, di, orr, oi in parts:
            bar_real = cross_real * dr + cross_imag * di - share * orr
            bar_imag = cross_real * di - cross_imag * dr - share * oi
            bars.append(jnp.concatenate([bar_real, bar_imag], 1))
    columns = const_right(jnp.concatenate(bars, 0), mixed_high, mixed_low)
    stacked = jnp.concatenate(
        [
            jnp.concatenate(
                [columns[f * HALF : (f + 1) * HALF, :SUB], columns[f * HALF : (f + 1) * HALF, SUB:]], 0
            )
            for f in range(FIELDS)
        ],
        1,
    )
    psf_bar = const_left(rows_high, rows_low, stacked) * (2.0 * scale)
    field_bar = jnp.concatenate([field[:SUB] * psf_bar, field[SUB:] * psf_bar], 0)
    half_bar = const_left(left_high, left_low, field_bar)
    q = PUP // 2
    rows = jnp.concatenate(
        [
            jnp.concatenate(
                [half_bar[n * q : (n + 1) * q, f * SUB : (f + 1) * SUB] for n in (0, 2, 1, 3)], 1
            )
            for f in range(FIELDS)
        ],
        0,
    )
    pupil_bar = const_right(rows, right_high, right_low)
    phase_bar = pupil[:, :SUB] * pupil_bar[:, SUB:] - pupil[:, SUB:] * pupil_bar[:, :SUB]
    size = FRAMES * q
    total = phase_bar[:size]
    for c in range(1, CH):
        total = total + phase_bar[c * size : (c + 1) * size] * np.float32(1.0 / (1.0 + 0.25 * c))
    modes = basis_ref.shape[0]
    ones = jnp.ones((8, SUB), F32)
    gap = jnp.zeros((1, SLOT - modes), F32)
    lines = []
    for f in range(FRAMES):
        part = jnp.sum(basis_ref[...] * total[f * q : (f + 1) * q][None], axis=1)
        line = lax.dot_general(
            ones, part, (((1,), (1,)), ((), ())), precision=HIGHEST, preferred_element_type=F32
        )
        lines += [line[:1], gap]
    return jnp.concatenate(
        [jnp.concatenate(lines[:4], 1), jnp.concatenate(lines[4:], 1)], 0
    )


def forward_kernel(scale, modes, coeff_ref, basis_ref, mask_ref, *refs):
    tables, (otf_ref, field_ref, pupil_ref) = refs[:8], refs[8:]
    otf, field, pupil = forward_math(scale, modes, coeff_ref, basis_ref, mask_ref, tables)
    otf_ref[0] = otf
    field_ref[0] = field
    pupil_ref[0] = pupil


def backward_kernel(scale, cells_ref, otf_ref, field_ref, pupil_ref, basis_ref, weight_ref, *refs):
    tables, data_tables, (data_ref, out_ref) = refs[:8], refs[8:12], refs[12:]
    images = jnp.concatenate(
        [cells_ref[:, 0, c, f].reshape(SUB, SUB) for c in range(CH) for f in range(FRAMES)], 1
    )
    data = half_plane(images, *data_tables)
    data_ref[0] = data
    out_ref[0] = backward_math(
        scale, data, otf_ref[0], field_ref[0], pupil_ref[0], basis_ref, weight_ref, tables
    )


def joint_kernel(scale, modes, coeff_ref, data_ref, basis_ref, mask_ref, weight_ref, *refs):
    forward_tables, backward_tables, out_ref = refs[:8], refs[8:16], refs[16]
    otf, field, pupil = forward_math(scale, modes, coeff_ref, basis_ref, mask_ref, forward_tables)
    out_ref[0] = backward_math(
        scale, data_ref[0], otf, field, pupil, basis_ref, weight_ref, backward_tables
    )


def gather_kernel(n, block_ref, out_ref, send_sem, recv_sem):
    me = lax.axis_index("sub")
    barrier = pltpu.get_barrier_semaphore()

    def greet(step, carry):
        pl.semaphore_signal(
            barrier,
            inc=1,
            device_id=(lax.rem(me + step, n),),
            device_id_type=pl.DeviceIdType.MESH,
        )
        return carry

    lax.fori_loop(1, n, greet, 0)
    pl.semaphore_wait(barrier, n - 1)

    def copy_to(step):
        return pltpu.make_async_remote_copy(
            src_ref=block_ref,
            dst_ref=out_ref.at[me],
            send_sem=send_sem.at[step],
            recv_sem=recv_sem.at[step],
            device_id=(lax.rem(me + step, n),),
            device_id_type=pl.DeviceIdType.MESH,
        )

    def begin(step, carry):
        copy_to(step).start()
        return carry

    def finish(step, carry):
        copy_to(step).wait()
        return carry

    lax.fori_loop(1, n, begin, 0)
    out_ref[me] = block_ref[...]
    lax.fori_loop(1, n, finish, 0)


def spread_blocks(block, ident):
    n = lax.axis_size("sub")
    return pl.pallas_call(
        functools.partial(gather_kernel, n),
        out_shape=jax.ShapeDtypeStruct((n,) + block.shape, F32),
        in_specs=[pl.BlockSpec(memory_space=pltpu.VMEM)],
        out_specs=pl.BlockSpec(memory_space=pltpu.VMEM),
        scratch_shapes=[pltpu.SemaphoreType.DMA((n,)), pltpu.SemaphoreType.DMA((n,))],
        compiler_params=pltpu.CompilerParams(collective_id=ident, has_side_effects=True),
    )(block)


def whole(array):
    return pl.BlockSpec(array.shape, lambda *_: (0,) * array.ndim, pipeline_mode=pl.Buffered(1))


def on_device(images, anchors, patches, coeffs, zbasis):
    devices = lax.axis_size("sub")
    device = lax.axis_index("sub")
    rows = images.shape[2]
    per = anchors.shape[0]
    owned = coeffs.shape[2]
    modes = coeffs.shape[1]
    tables = make_tables()
    pairs = {
        name: [jnp.asarray(part) for part in split_np(tables[name])]
        for name in tables
        if name not in ("weight", "mask", "area")
    }
    twice = {
        name: [jnp.concatenate([pairs[name][0]] * 2, 1), pairs[name][1]]
        for name in ("left", "rows", "data_rows")
    }
    scale = float(1.0 / (SUB * SUB * tables["area"]))

    owned_rows = owned * 2
    tile_rows = -(-(owned_rows + 2) // 8) * 8
    mine = jnp.zeros((tile_rows, SUB), F32)
    packed = coeffs.transpose(2, 0, 1).reshape(owned_rows, 2, modes)
    packed = jnp.pad(packed, ((0, 0), (0, 0), (0, SLOT - modes))).reshape(owned_rows, SUB)
    mine = mine.at[:owned_rows].set(packed)
    owned_row_patch = owned_rows
    mine = mine.at[owned_rows, :per].set(patches.astype(F32))
    mine = mine.at[owned_rows + 1, :per].set(anchors.astype(F32))
    everyone = spread_blocks(mine, 0)
    all_coeffs = everyone[:, :owned_rows, :].reshape(devices * owned, 2 * SUB)
    group = devices // TR
    tile = device // group
    place = device % group
    share = devices * per // TR // group
    all_patches = everyone[:, owned_row_patch, :per].reshape(devices * per // TR, TR)
    all_anchors = everyone[:, owned_row_patch + 1, :per].reshape(devices * per // TR, TR)
    all_patches = all_patches.astype(jnp.int32).T
    pick_tile = (jnp.arange(TR, dtype=jnp.int32) == tile)[None, :]
    tile_anchors = jnp.sum(jnp.where(pick_tile, all_anchors, 0.0), axis=1).astype(jnp.int32)
    patches = lax.dynamic_slice(all_patches, (tile, place * share), (1, share)).reshape(share)
    all_patches = all_patches.reshape(devices * per)

    count = devices * per // TR
    batch = 8
    bands = images.reshape(CH * FRAMES * rows, images.shape[3])
    windows = pl.pallas_call(
        functools.partial(window_kernel, batch),
        grid_spec=pltpu.PrefetchScalarGridSpec(
            num_scalar_prefetch=1,
            grid=(count // batch,),
            in_specs=[pl.BlockSpec(bands.shape, lambda j, a: (0, 0), pipeline_mode=pl.Buffered(1))],
            out_specs=pl.BlockSpec((batch, bands.shape[0], SUB), lambda j, a: (j, 0, 0)),
        ),
        out_shape=jax.ShapeDtypeStruct((count, bands.shape[0], SUB), F32),
        compiler_params=pltpu.CompilerParams(vmem_limit_bytes=VMEM_LIMIT),
    )(tile_anchors, bands)
    teams = [list(range(g * group, (g + 1) * group)) for g in range(TR)]
    received = lax.all_to_all(windows, "sub", 0, 0, axis_index_groups=teams, tiled=True)
    cells = received.reshape(group, share, CH, FRAMES, rows, SUB)
    if rows % 8:
        cells = cells.transpose(1, 2, 3, 0, 4, 5).reshape(1, share, CH, FRAMES, SUB, SUB)
    per = share

    big = pltpu.CompilerParams(vmem_limit_bytes=VMEM_LIMIT)
    basis = zbasis.reshape(modes, PUP // 2, SUB)
    mask = jnp.asarray(tables["mask"])
    weight = jnp.asarray(tables["weight"])
    forward_tables = pairs["right"] + twice["left"] + twice["rows"] + pairs["mixed"]
    backward_tables = pairs["mixed"] + pairs["rows_t"] + pairs["left_t"] + pairs["right_t"]
    data_tables = twice["data_rows"] + pairs["data_mixed"]
    saved_shapes = [
        jax.ShapeDtypeStruct((per, FIELDS * HALF, 2 * SUB), F32),
        jax.ShapeDtypeStruct((per, 2 * SUB, FIELDS * SUB), F32),
        jax.ShapeDtypeStruct((per, FIELDS * PUP // 2, 2 * SUB), F32),
    ]
    saved_specs = [pl.BlockSpec((1,) + t.shape[1:], lambda s: (s, 0, 0)) for t in saved_shapes]
    slope_shape = jax.ShapeDtypeStruct((per, 2, SUB), F32)
    slope_spec = pl.BlockSpec((1, 2, SUB), lambda s: (s, 0, 0))
    smem = pl.BlockSpec(memory_space=pltpu.SMEM)

    def cost(flops):
        return pl.CostEstimate(flops=flops, bytes_accessed=8 << 20, transcendentals=0)

    def first_slopes(chosen):
        saved = pl.pallas_call(
            functools.partial(forward_kernel, scale, modes),
            grid=(per,),
            in_specs=[smem, whole(basis), whole(mask)] + [whole(t) for t in forward_tables],
            out_specs=saved_specs,
            out_shape=saved_shapes,
            compiler_params=big,
            cost_estimate=cost(10**10),
        )(chosen.reshape(per * 2, SUB), basis, mask, *forward_tables)
        cell_spec = pl.BlockSpec(
            (cells.shape[0], 1) + cells.shape[2:], lambda s: (0, s, 0, 0, 0, 0)
        )
        return pl.pallas_call(
            functools.partial(backward_kernel, scale),
            grid=(per,),
            in_specs=[cell_spec]
            + saved_specs
            + [whole(t) for t in [basis, weight] + backward_tables + data_tables],
            out_specs=[saved_specs[0], slope_spec],
            out_shape=[saved_shapes[0], slope_shape],
            compiler_params=big,
            cost_estimate=cost(10**10),
        )(cells, *saved, basis, weight, *backward_tables, *data_tables)

    def later_slopes(chosen, data):
        fixed = [basis, mask, weight] + forward_tables + backward_tables
        return pl.pallas_call(
            functools.partial(joint_kernel, scale, modes),
            grid=(per,),
            in_specs=[smem, saved_specs[0]] + [whole(t) for t in fixed],
            out_specs=slope_spec,
            out_shape=slope_shape,
            compiler_params=big,
            cost_estimate=cost(2 * 10**10),
        )(chosen.reshape(per * 2, SUB), data, *fixed)

    patch_ids = jnp.arange(devices * owned, dtype=jnp.int32)
    own_ids = device * owned + jnp.arange(owned, dtype=jnp.int32)
    wanted = jnp.concatenate([patches, own_ids])
    picks = (wanted[:, None] == patch_ids[None, :]).astype(F32)
    current = jnp.dot(picks, all_coeffs, precision=HIGHEST)
    sums = (wanted[:, None] == all_patches[None, :]).astype(F32)
    gradient = jnp.zeros_like(current)
    for iteration in range(ITERS):
        if iteration == 0:
            data, slopes = first_slopes(current[:per])
        else:
            slopes = later_slopes(current[:per], data)
        gathered = spread_blocks(slopes.reshape(per * 2, SUB), 1 + iteration)
        gathered = gathered.reshape(devices * per, 2 * SUB)
        gradient = jnp.dot(sums, gathered, precision=HIGHEST)
        current = current - STEP_SIZE * gradient

    def owned_part(value):
        return value[per:].reshape(owned, FRAMES, SLOT)[:, :, :modes].transpose(1, 2, 0)

    return owned_part(current), owned_part(gradient)


def solution(mesh):
    return jax.shard_map(
        on_device,
        mesh=mesh,
        in_specs=(P(None, None, "sub", None), P("sub"), P("sub"), P(None, None, "sub"), P()),
        out_specs=(P(None, None, "sub"), P(None, None, "sub")),
        check_vma=False,
    )
```

```python
import functools
import math

import jax
import jax.numpy as jnp
import ml_dtypes
import numpy as np
from jax import lax
from jax.experimental import pallas as pl
from jax.experimental.pallas import tpu as pltpu
from jax.sharding import PartitionSpec as P

SUB = 128
CH = 2
FRAMES = 4
FIELDS = CH * FRAMES
SLOT = 64
TR = 4
ITERS = 2
PUP = 64
HALF = 72
GAMMA = 0.01
STEP_SIZE = 0.05
F32 = jnp.float32
BF16 = jnp.bfloat16
VMEM_LIMIT = 48 << 20
HIGHEST = lax.Precision.HIGHEST


def split_np(matrix):
    matrix = np.asarray(matrix, np.float32)
    high = matrix.astype(ml_dtypes.bfloat16)
    low = (matrix - high.astype(np.float32)).astype(ml_dtypes.bfloat16)
    return high, low


def make_tables():
    k = np.arange(SUB)
    angle = 2.0 * np.pi * (np.outer(k, k) % SUB) / SUB
    cos, sin = np.cos(angle), np.sin(angle)
    taper = 0.5 - 0.5 * np.cos(2.0 * np.pi * (k + 0.5) / SUB)
    right = np.zeros((2, 2, PUP, 2, 2, SUB))
    for half in range(2):
        right[0, half, :, half, 0] = cos[:PUP]
        right[0, half, :, half, 1] = -sin[:PUP]
        right[1, half, :, half, 0] = sin[:PUP]
        right[1, half, :, half, 1] = cos[:PUP]
    right = right.reshape(2 * SUB, 4 * SUB)
    left = np.block([[cos[:, :PUP], sin[:, :PUP]], [-sin[:, :PUP], cos[:, :PUP]]])
    left = left.reshape(2 * SUB, 2, PUP // 2, 2).transpose(0, 1, 3, 2).reshape(2 * SUB, SUB)
    rows_cos, rows_sin = np.zeros((HALF, SUB)), np.zeros((HALF, SUB))
    rows_cos[:65], rows_sin[:65] = cos[:65], sin[:65]
    rows = np.concatenate([rows_cos, rows_sin], 0)
    mixed = np.block([[cos, -sin], [-sin, -cos]])
    weight = np.zeros((HALF, 1))
    weight[:65] = 2.0
    weight[0] = weight[64] = 1.0
    centred = np.arange(PUP) - PUP / 2 + 0.5
    mask = (centred[:, None] ** 2 + centred[None, :] ** 2 <= (PUP / 2) ** 2).astype(np.float32)
    area = float(mask.sum())
    mask = mask.reshape(PUP // 2, SUB)
    return {
        "right": right,
        "right_t": right.T,
        "left": left,
        "left_t": left.T,
        "rows": rows,
        "rows_t": rows.T,
        "mixed": mixed,
        "data_rows": rows * taper[None, :],
        "data_mixed": np.concatenate([taper, taper])[:, None] * mixed,
        "weight": np.broadcast_to(weight, (HALF, SUB)).astype(np.float32) * np.float32(-2.0 / SUB**4),
        "mask": mask,
        "area": area,
    }


def pack_tables(tables):
    split_tables = {name: split_np(tables[name]) for name in tables if name not in ("weight", "mask", "area")}
    for half in range(2):
        split_tables["right%d" % half] = tuple(
            part[:, half * 2 * SUB : (half + 1) * 2 * SUB] for part in split_tables["right"]
        )
    del split_tables["right"]
    for name in ("left", "rows", "data_rows"):
        high, low = split_tables[name]
        split_tables[name] = (np.concatenate([high, high], 1), low)
    spots, parts, at = {}, [], 0
    for name in sorted(split_tables):
        for part in split_tables[name]:
            spots.setdefault(name, []).append((at, part.shape[0], part.shape[1]))
            parts.append(np.pad(part, ((0, 0), (0, 2 * SUB - part.shape[1]))))
            at += part.shape[0]
    return np.concatenate(parts, 0), spots


def views(ref, spots, *names):
    return [ref.at[pl.ds(at, size), pl.ds(0, width)] for name in names for at, size, width in spots[name]]


def split(value):
    high = value.astype(BF16)
    low = (value - high.astype(F32)).astype(BF16)
    return high, low


def dot(a, b):
    return jnp.dot(a, b, preferred_element_type=F32)


def const_left(high_ref, low_ref, value):
    high, low = split(value)
    table = high_ref[...]
    return dot(table, high) + (dot(table, low) + dot(low_ref[...], high))


def const_right(value, high_ref, low_ref):
    high, low = split(value)
    table = high_ref[...]
    return dot(high, table) + (dot(low, table) + dot(high, low_ref[...]))


def sin_cos(angle):
    turns = jnp.floor(angle * np.float32(2.0 / math.pi) + 0.5)
    rest = angle - turns * np.float32(1.5703125)
    rest = rest - turns * np.float32(4.8351287841796875e-4)
    rest = rest - turns * np.float32(3.1385570764541626e-7)
    rest = rest - turns * np.float32(6.0771005065061922e-11)
    square = rest * rest
    sine = rest + rest * square * (
        -1.6666654611e-1 + square * (8.3321608736e-3 + square * -1.9515295891e-4)
    )
    cosine = 1.0 - 0.5 * square + square * square * (
        4.166664568298827e-2 + square * (-1.388731625493765e-3 + square * 2.443315711809948e-5)
    )
    quadrant = turns - 4.0 * jnp.floor(turns * 0.25)
    odd = (quadrant == 1.0) | (quadrant == 3.0)
    base_sin = jnp.where(odd, cosine, sine)
    base_cos = jnp.where(odd, sine, cosine)
    out_sin = jnp.where(quadrant >= 2.0, -base_sin, base_sin)
    out_cos = jnp.where((quadrant == 1.0) | (quadrant == 2.0), -base_cos, base_cos)
    return out_sin, out_cos


def stacked_left(twice_ref, low_ref, value):
    high, low = split(value)
    return dot(twice_ref[...], jnp.concatenate([high, low], 0)) + dot(low_ref[...], high)


def half_plane(images, rows_twice, rows_low, mixed_high, mixed_low):
    columns = stacked_left(rows_twice, rows_low, images)
    stacked = jnp.concatenate(
        [
            jnp.concatenate(
                [columns[:HALF, f * SUB : (f + 1) * SUB], columns[HALF:, f * SUB : (f + 1) * SUB]], 1
            )
            for f in range(FIELDS)
        ],
        0,
    )
    return const_right(stacked, mixed_high, mixed_low)


def window_kernel(batch, anchor_ref, image_ref, out_ref):
    last = image_ref.shape[1] - SUB
    lane = lax.broadcasted_iota(jnp.int32, (image_ref.shape[0], SUB), 1)
    for k in range(batch):
        anchor = anchor_ref[pl.program_id(0) * batch + k]
        base = pl.multiple_of((anchor // SUB) * SUB, SUB)
        after = pl.multiple_of(jnp.minimum(base + SUB, last), SUB)
        shift = anchor - base
        turn = lax.rem(SUB - shift, SUB)
        first = pltpu.roll(image_ref[:, pl.ds(base, SUB)], turn, 1)
        second = pltpu.roll(image_ref[:, pl.ds(after, SUB)], turn, 1)
        reach = jnp.where(base + SUB <= last, SUB, 0)
        out_ref[k] = jnp.where(
            lane < SUB - shift, first, jnp.where(lane < reach, second, 0.0)
        )


def forward_math(scale, modes, coeff_ref, basis_ref, mask_ref, tables):
    left_twice, left_low, rows_twice, rows_low, mixed_high, mixed_low = tables[4:]
    subfield = pl.program_id(0)
    q = PUP // 2
    sums = [jnp.zeros((q, SUB), F32) for _ in range(FRAMES)]
    for m in range(modes):
        mode = basis_ref[m]
        for f in range(FRAMES):
            value = coeff_ref[subfield * 2 + f // 2, (f % 2) * SLOT + m]
            sums[f] = sums[f] + value * mode
    phase = jnp.concatenate(sums, 0)
    phase = jnp.concatenate([phase * np.float32(1.0 / (1.0 + 0.25 * c)) for c in range(CH)], 0)
    sine, cosine = sin_cos(phase)
    mask = jnp.concatenate([mask_ref[:q]] * FIELDS, 0)
    pupil = jnp.concatenate([mask * cosine, mask * sine], 1)
    half = jnp.concatenate([const_right(pupil, *tables[:2]), const_right(pupil, *tables[2:4])], 1)
    blocks = jnp.concatenate(
        [
            jnp.concatenate(
                [half[f * q : (f + 1) * q, n * SUB : (n + 1) * SUB] for n in (0, 2, 1, 3)], 0
            )
            for f in range(FIELDS)
        ],
        1,
    )
    field = stacked_left(left_twice, left_low, blocks)
    psf = (field[:SUB] * field[:SUB] + field[SUB:] * field[SUB:]) * scale
    return half_plane(psf, rows_twice, rows_low, mixed_high, mixed_low), field, pupil


def backward_math(scale, data, otf, field, pupil, basis_ref, weight_ref, tables):
    mixed_high, mixed_low, rows_high, rows_low, left_high, left_low, right_high, right_low = tables
    weight = weight_ref[PUP // 2 :]
    bars = []
    for c in range(CH):
        parts = []
        cross_real = cross_imag = power = None
        for f in range(c * FRAMES, (c + 1) * FRAMES):
            d, o = data[f * HALF : (f + 1) * HALF], otf[f * HALF : (f + 1) * HALF]
            dr, di, orr, oi = d[:, :SUB], d[:, SUB:], o[:, :SUB], o[:, SUB:]
            parts.append((dr, di, orr, oi))
            terms = (dr * orr + di * oi, di * orr - dr * oi, orr * orr + oi * oi)
            if cross_real is None:
                cross_real, cross_imag, power = terms
            else:
                cross_real = cross_real + terms[0]
                cross_imag = cross_imag + terms[1]
                power = power + terms[2]
        inverse = 1.0 / (power + GAMMA)
        slope = weight * inverse
        xr, xi = cross_real * inverse, cross_imag * inverse
        share = weight * (xr * xr + xi * xi)
        cross_real, cross_imag = cross_real * slope, cross_imag * slope
        for dr, di, orr, oi in parts:
            bar_real = cross_real * dr + cross_imag * di - share * orr
            bar_imag = cross_real * di - cross_imag * dr - share * oi
            bars.append(jnp.concatenate([bar_real, bar_imag], 1))
    columns = const_right(jnp.concatenate(bars, 0), mixed_high, mixed_low)
    stacked = jnp.concatenate(
        [
            jnp.concatenate(
                [columns[f * HALF : (f + 1) * HALF, :SUB], columns[f * HALF : (f + 1) * HALF, SUB:]], 0
            )
            for f in range(FIELDS)
        ],
        1,
    )
    psf_bar = const_left(rows_high, rows_low, stacked) * (2.0 * scale)
    field_bar = jnp.concatenate([field[:SUB] * psf_bar, field[SUB:] * psf_bar], 0)
    half_bar = const_left(left_high, left_low, field_bar)
    q = PUP // 2
    rows = jnp.concatenate(
        [
            jnp.concatenate(
                [half_bar[n * q : (n + 1) * q, f * SUB : (f + 1) * SUB] for n in (0, 2, 1, 3)], 1
            )
            for f in range(FIELDS)
        ],
        0,
    )
    pupil_bar = const_right(rows, right_high, right_low)
    phase_bar = pupil[:, :SUB] * pupil_bar[:, SUB:] - pupil[:, SUB:] * pupil_bar[:, :SUB]
    size = FRAMES * q
    total = phase_bar[:size]
    for c in range(1, CH):
        total = total + phase_bar[c * size : (c + 1) * size] * np.float32(1.0 / (1.0 + 0.25 * c))
    modes = basis_ref.shape[0]
    ones = jnp.ones((8, SUB), F32)
    gap = jnp.zeros((1, SLOT - modes), F32)
    lines = []
    for f in range(FRAMES):
        part = jnp.sum(basis_ref[...] * total[f * q : (f + 1) * q][None], axis=1)
        line = lax.dot_general(
            ones, part, (((1,), (1,)), ((), ())), precision=HIGHEST, preferred_element_type=F32
        )
        lines += [line[:1], gap]
    return jnp.concatenate(
        [jnp.concatenate(lines[:4], 1), jnp.concatenate(lines[4:], 1)], 0
    )


FORWARD = ("right0", "right1", "left", "rows", "mixed")
BACKWARD = ("mixed", "rows_t", "left_t", "right_t")
DATA = ("data_rows", "data_mixed")


def forward_kernel(scale, modes, spots, coeff_ref, basis_ref, fixed_ref, pack_ref, otf_ref, field_ref, pupil_ref):
    tables = views(pack_ref, spots, *FORWARD)
    otf, field, pupil = forward_math(scale, modes, coeff_ref, basis_ref, fixed_ref, tables)
    otf_ref[0] = otf
    field_ref[0] = field
    pupil_ref[0] = pupil


def backward_kernel(
    scale, spots, cells_ref, otf_ref, field_ref, pupil_ref, basis_ref, fixed_ref, pack_ref, data_ref, out_ref
):
    images = jnp.concatenate(
        [cells_ref[:, 0, c, f].reshape(SUB, SUB) for c in range(CH) for f in range(FRAMES)], 1
    )
    data = half_plane(images, *views(pack_ref, spots, *DATA))
    data_ref[0] = data
    tables = views(pack_ref, spots, *BACKWARD)
    out_ref[0] = backward_math(
        scale, data, otf_ref[0], field_ref[0], pupil_ref[0], basis_ref, fixed_ref, tables
    )


def joint_kernel(scale, modes, spots, coeff_ref, data_ref, basis_ref, fixed_ref, pack_ref, out_ref):
    tables = views(pack_ref, spots, *FORWARD)
    otf, field, pupil = forward_math(scale, modes, coeff_ref, basis_ref, fixed_ref, tables)
    tables = views(pack_ref, spots, *BACKWARD)
    out_ref[0] = backward_math(scale, data_ref[0], otf, field, pupil, basis_ref, fixed_ref, tables)


def gather_kernel(n, block_ref, out_ref, send_sem, recv_sem):
    me = lax.axis_index("sub")
    barrier = pltpu.get_barrier_semaphore()

    def greet(step, carry):
        pl.semaphore_signal(
            barrier,
            inc=1,
            device_id=(lax.rem(me + step, n),),
            device_id_type=pl.DeviceIdType.MESH,
        )
        return carry

    lax.fori_loop(1, n, greet, 0)
    pl.semaphore_wait(barrier, n - 1)

    def copy_to(step):
        return pltpu.make_async_remote_copy(
            src_ref=block_ref,
            dst_ref=out_ref.at[me],
            send_sem=send_sem.at[step],
            recv_sem=recv_sem.at[step],
            device_id=(lax.rem(me + step, n),),
            device_id_type=pl.DeviceIdType.MESH,
        )

    def begin(step, carry):
        copy_to(step).start()
        return carry

    def finish(step, carry):
        copy_to(step).wait()
        return carry

    lax.fori_loop(1, n, begin, 0)
    out_ref[me] = block_ref[...]
    lax.fori_loop(1, n, finish, 0)


def spread_blocks(block, ident):
    n = lax.axis_size("sub")
    return pl.pallas_call(
        functools.partial(gather_kernel, n),
        out_shape=jax.ShapeDtypeStruct((n,) + block.shape, F32),
        in_specs=[pl.BlockSpec(memory_space=pltpu.VMEM)],
        out_specs=pl.BlockSpec(memory_space=pltpu.VMEM),
        scratch_shapes=[pltpu.SemaphoreType.DMA((n,)), pltpu.SemaphoreType.DMA((n,))],
        compiler_params=pltpu.CompilerParams(collective_id=ident, has_side_effects=True),
    )(block)


def whole(array):
    return pl.BlockSpec(array.shape, lambda *_: (0,) * array.ndim, pipeline_mode=pl.Buffered(1))


def on_device(images, anchors, patches, coeffs, zbasis):
    devices = lax.axis_size("sub")
    device = lax.axis_index("sub")
    rows = images.shape[2]
    per = anchors.shape[0]
    owned = coeffs.shape[2]
    modes = coeffs.shape[1]
    tables = make_tables()
    pack, spots = pack_tables(tables)
    pack = jnp.asarray(pack)
    scale = float(1.0 / (SUB * SUB * tables["area"]))

    owned_rows = owned * 2
    tile_rows = -(-(owned_rows + 2) // 8) * 8
    mine = jnp.zeros((tile_rows, SUB), F32)
    packed = coeffs.transpose(2, 0, 1).reshape(owned_rows, 2, modes)
    packed = jnp.pad(packed, ((0, 0), (0, 0), (0, SLOT - modes))).reshape(owned_rows, SUB)
    mine = mine.at[:owned_rows].set(packed)
    owned_row_patch = owned_rows
    mine = mine.at[owned_rows, :per].set(patches.astype(F32))
    mine = mine.at[owned_rows + 1, :per].set(anchors.astype(F32))
    everyone = spread_blocks(mine, 0)
    all_coeffs = everyone[:, :owned_rows, :].reshape(devices * owned, 2 * SUB)
    group = devices // TR
    tile = device // group
    place = device % group
    share = devices * per // TR // group
    all_patches = everyone[:, owned_row_patch, :per].reshape(devices * per // TR, TR)
    all_anchors = everyone[:, owned_row_patch + 1, :per].reshape(devices * per // TR, TR)
    all_patches = all_patches.astype(jnp.int32).T
    pick_tile = (jnp.arange(TR, dtype=jnp.int32) == tile)[None, :]
    tile_anchors = jnp.sum(jnp.where(pick_tile, all_anchors, 0.0), axis=1).astype(jnp.int32)
    patches = lax.dynamic_slice(all_patches, (tile, place * share), (1, share)).reshape(share)
    all_patches = all_patches.reshape(devices * per)

    count = devices * per // TR
    batch = 8
    bands = images.reshape(CH * FRAMES * rows, images.shape[3])
    windows = pl.pallas_call(
        functools.partial(window_kernel, batch),
        grid_spec=pltpu.PrefetchScalarGridSpec(
            num_scalar_prefetch=1,
            grid=(count // batch,),
            in_specs=[pl.BlockSpec(bands.shape, lambda j, a: (0, 0), pipeline_mode=pl.Buffered(1))],
            out_specs=pl.BlockSpec((batch, bands.shape[0], SUB), lambda j, a: (j, 0, 0)),
        ),
        out_shape=jax.ShapeDtypeStruct((count, bands.shape[0], SUB), F32),
        compiler_params=pltpu.CompilerParams(vmem_limit_bytes=VMEM_LIMIT),
    )(tile_anchors, bands)
    teams = [list(range(g * group, (g + 1) * group)) for g in range(TR)]
    received = lax.all_to_all(windows, "sub", 0, 0, axis_index_groups=teams, tiled=True)
    cells = received.reshape(group, share, CH, FRAMES, rows, SUB)
    if rows % 8:
        cells = cells.transpose(1, 2, 3, 0, 4, 5).reshape(1, share, CH, FRAMES, SUB, SUB)
    per = share

    big = pltpu.CompilerParams(vmem_limit_bytes=VMEM_LIMIT)
    basis = zbasis.reshape(modes, PUP // 2, SUB)
    fixed = jnp.asarray(np.concatenate([tables["mask"], tables["weight"]], 0))
    shared = [basis, fixed, pack]
    saved_shapes = [
        jax.ShapeDtypeStruct((per, FIELDS * HALF, 2 * SUB), F32),
        jax.ShapeDtypeStruct((per, 2 * SUB, FIELDS * SUB), F32),
        jax.ShapeDtypeStruct((per, FIELDS * PUP // 2, 2 * SUB), F32),
    ]
    saved_specs = [pl.BlockSpec((1,) + t.shape[1:], lambda s: (s, 0, 0)) for t in saved_shapes]
    slope_shape = jax.ShapeDtypeStruct((per, 2, SUB), F32)
    slope_spec = pl.BlockSpec((1, 2, SUB), lambda s: (s, 0, 0))
    smem = pl.BlockSpec(memory_space=pltpu.SMEM)

    def cost(flops):
        return pl.CostEstimate(flops=flops, bytes_accessed=8 << 20, transcendentals=0)

    def first_slopes(chosen):
        saved = pl.pallas_call(
            functools.partial(forward_kernel, scale, modes, spots),
            grid=(per,),
            in_specs=[smem] + [whole(t) for t in shared],
            out_specs=saved_specs,
            out_shape=saved_shapes,
            compiler_params=big,
            cost_estimate=cost(10**10),
        )(chosen.reshape(per * 2, SUB), *shared)
        cell_spec = pl.BlockSpec(
            (cells.shape[0], 1) + cells.shape[2:], lambda s: (0, s, 0, 0, 0, 0)
        )
        return pl.pallas_call(
            functools.partial(backward_kernel, scale, spots),
            grid=(per,),
            in_specs=[cell_spec]
            + saved_specs
            + [whole(t) for t in shared],
            out_specs=[saved_specs[0], slope_spec],
            out_shape=[saved_shapes[0], slope_shape],
            compiler_params=big,
            cost_estimate=cost(10**10),
        )(cells, *saved, *shared)

    def later_slopes(chosen, data):
        return pl.pallas_call(
            functools.partial(joint_kernel, scale, modes, spots),
            grid=(per,),
            in_specs=[smem, saved_specs[0]] + [whole(t) for t in shared],
            out_specs=slope_spec,
            out_shape=slope_shape,
            compiler_params=big,
            cost_estimate=cost(2 * 10**10),
        )(chosen.reshape(per * 2, SUB), data, *shared)

    patch_ids = jnp.arange(devices * owned, dtype=jnp.int32)
    own_ids = device * owned + jnp.arange(owned, dtype=jnp.int32)
    wanted = jnp.concatenate([patches, own_ids])
    picks = (wanted[:, None] == patch_ids[None, :]).astype(F32)
    current = jnp.dot(picks, all_coeffs, precision=HIGHEST)
    sums = (wanted[:, None] == all_patches[None, :]).astype(F32)
    gradient = jnp.zeros_like(current)
    for iteration in range(ITERS):
        if iteration == 0:
            data, slopes = first_slopes(current[:per])
        else:
            slopes = later_slopes(current[:per], data)
        gathered = spread_blocks(slopes.reshape(per * 2, SUB), 1 + iteration)
        gathered = gathered.reshape(devices * per, 2 * SUB)
        gradient = jnp.dot(sums, gathered, precision=HIGHEST)
        current = current - STEP_SIZE * gradient

    def owned_part(value):
        return value[per:].reshape(owned, FRAMES, SLOT)[:, :, :modes].transpose(1, 2, 0)

    return owned_part(current), owned_part(gradient)


def solution(mesh):
    return jax.shard_map(
        on_device,
        mesh=mesh,
        in_specs=(P(None, None, "sub", None), P("sub"), P("sub"), P(None, None, "sub"), P()),
        out_specs=(P(None, None, "sub"), P(None, None, "sub")),
        check_vma=False,
    )
```

```python
import functools
import math

import jax
import jax.numpy as jnp
import ml_dtypes
import numpy as np
from jax import lax
from jax.experimental import pallas as pl
from jax.experimental.pallas import tpu as pltpu
from jax.sharding import PartitionSpec as P

SUB = 128
CH = 2
FRAMES = 4
FIELDS = CH * FRAMES
SLOT = 64
TR = 4
ITERS = 2
PUP = 64
HALF = 72
GAMMA = 0.01
STEP_SIZE = 0.05
F32 = jnp.float32
BF16 = jnp.bfloat16
VMEM_LIMIT = 48 << 20
HIGHEST = lax.Precision.HIGHEST


def split_np(matrix):
    matrix = np.asarray(matrix, np.float32)
    high = matrix.astype(ml_dtypes.bfloat16)
    low = (matrix - high.astype(np.float32)).astype(ml_dtypes.bfloat16)
    return high, low


def make_tables():
    k = np.arange(SUB)
    angle = 2.0 * np.pi * (np.outer(k, k) % SUB) / SUB
    cos, sin = np.cos(angle), np.sin(angle)
    taper = 0.5 - 0.5 * np.cos(2.0 * np.pi * (k + 0.5) / SUB)
    right = np.zeros((2, 2, PUP, 2, 2, SUB))
    for half in range(2):
        right[0, half, :, half, 0] = cos[:PUP]
        right[0, half, :, half, 1] = -sin[:PUP]
        right[1, half, :, half, 0] = sin[:PUP]
        right[1, half, :, half, 1] = cos[:PUP]
    right = right.reshape(2 * SUB, 4 * SUB)
    left = np.block([[cos[:, :PUP], sin[:, :PUP]], [-sin[:, :PUP], cos[:, :PUP]]])
    left = left.reshape(2 * SUB, 2, PUP // 2, 2).transpose(0, 1, 3, 2).reshape(2 * SUB, SUB)
    rows_cos, rows_sin = np.zeros((HALF, SUB)), np.zeros((HALF, SUB))
    rows_cos[:65], rows_sin[:65] = cos[:65], sin[:65]
    rows = np.concatenate([rows_cos, rows_sin], 0)
    mixed = np.block([[cos, -sin], [-sin, -cos]])
    weight = np.zeros((HALF, 1))
    weight[:65] = 2.0
    weight[0] = weight[64] = 1.0
    centred = np.arange(PUP) - PUP / 2 + 0.5
    mask = (centred[:, None] ** 2 + centred[None, :] ** 2 <= (PUP / 2) ** 2).astype(np.float32)
    area = float(mask.sum())
    mask = mask.reshape(PUP // 2, SUB)
    return {
        "right": right,
        "right_t": right.T,
        "left": left,
        "left_t": left.T,
        "rows": rows,
        "rows_t": rows.T,
        "mixed": mixed,
        "data_rows": rows * taper[None, :],
        "data_mixed": np.concatenate([taper, taper])[:, None] * mixed,
        "weight": np.broadcast_to(weight, (HALF, SUB)).astype(np.float32) * np.float32(-2.0 / SUB**4),
        "mask": mask,
        "area": area,
    }


def pack_tables(tables):
    split_tables = {name: split_np(tables[name]) for name in tables if name not in ("weight", "mask", "area")}
    for half in range(2):
        split_tables["right%d" % half] = tuple(
            part[:, half * 2 * SUB : (half + 1) * 2 * SUB] for part in split_tables["right"]
        )
    del split_tables["right"]
    for name in ("left", "rows", "data_rows"):
        high, low = split_tables[name]
        split_tables[name] = (np.concatenate([high, high], 1), low)
    spots, parts, at = {}, [], 0
    for name in sorted(split_tables):
        for part in split_tables[name]:
            spots.setdefault(name, []).append((at, part.shape[0], part.shape[1]))
            parts.append(np.pad(part, ((0, 0), (0, 2 * SUB - part.shape[1]))))
            at += part.shape[0]
    return np.concatenate(parts, 0), spots


def views(ref, spots, *names):
    return [ref.at[pl.ds(at, size), pl.ds(0, width)] for name in names for at, size, width in spots[name]]


def split(value):
    high = value.astype(BF16)
    low = (value - high.astype(F32)).astype(BF16)
    return high, low


def dot(a, b):
    return jnp.dot(a, b, preferred_element_type=F32)


def const_left(high_ref, low_ref, value):
    high, low = split(value)
    table = high_ref[...]
    return dot(table, high) + (dot(table, low) + dot(low_ref[...], high))


def const_right(value, high_ref, low_ref):
    high, low = split(value)
    table = high_ref[...]
    return dot(high, table) + (dot(low, table) + dot(high, low_ref[...]))


def sin_cos(angle):
    turns = jnp.floor(angle * np.float32(2.0 / math.pi) + 0.5)
    rest = angle - turns * np.float32(1.5703125)
    rest = rest - turns * np.float32(4.8351287841796875e-4)
    rest = rest - turns * np.float32(3.1385570764541626e-7)
    rest = rest - turns * np.float32(6.0771005065061922e-11)
    square = rest * rest
    sine = rest + rest * square * (
        -1.6666654611e-1 + square * (8.3321608736e-3 + square * -1.9515295891e-4)
    )
    cosine = 1.0 - 0.5 * square + square * square * (
        4.166664568298827e-2 + square * (-1.388731625493765e-3 + square * 2.443315711809948e-5)
    )
    quadrant = turns - 4.0 * jnp.floor(turns * 0.25)
    odd = (quadrant == 1.0) | (quadrant == 3.0)
    base_sin = jnp.where(odd, cosine, sine)
    base_cos = jnp.where(odd, sine, cosine)
    out_sin = jnp.where(quadrant >= 2.0, -base_sin, base_sin)
    out_cos = jnp.where((quadrant == 1.0) | (quadrant == 2.0), -base_cos, base_cos)
    return out_sin, out_cos


def stacked_left(twice_ref, low_ref, value):
    high, low = split(value)
    return dot(twice_ref[...], jnp.concatenate([high, low], 0)) + dot(low_ref[...], high)


def half_plane(images, rows_twice, rows_low, mixed_high, mixed_low):
    columns = stacked_left(rows_twice, rows_low, images)
    stacked = jnp.concatenate(
        [
            jnp.concatenate(
                [columns[:HALF, f * SUB : (f + 1) * SUB], columns[HALF:, f * SUB : (f + 1) * SUB]], 1
            )
            for f in range(FIELDS)
        ],
        0,
    )
    return const_right(stacked, mixed_high, mixed_low)


def window_kernel(batch, anchor_ref, image_ref, out_ref):
    last = image_ref.shape[1] - SUB
    lane = lax.broadcasted_iota(jnp.int32, (image_ref.shape[0], SUB), 1)
    for k in range(batch):
        anchor = anchor_ref[pl.program_id(0) * batch + k]
        base = pl.multiple_of((anchor // SUB) * SUB, SUB)
        after = pl.multiple_of(jnp.minimum(base + SUB, last), SUB)
        shift = anchor - base
        turn = lax.rem(SUB - shift, SUB)
        first = pltpu.roll(image_ref[:, pl.ds(base, SUB)], turn, 1)
        second = pltpu.roll(image_ref[:, pl.ds(after, SUB)], turn, 1)
        reach = jnp.where(base + SUB <= last, SUB, 0)
        out_ref[k] = jnp.where(
            lane < SUB - shift, first, jnp.where(lane < reach, second, 0.0)
        )


def forward_math(scale, modes, coeff_ref, basis_ref, mask_ref, tables):
    left_twice, left_low, rows_twice, rows_low, mixed_high, mixed_low = tables[4:]
    subfield = pl.program_id(0)
    q = PUP // 2
    sums = [jnp.zeros((q, SUB), F32) for _ in range(FRAMES)]
    for m in range(modes):
        mode = basis_ref[m]
        for f in range(FRAMES):
            value = coeff_ref[subfield * 2 + f // 2, (f % 2) * SLOT + m]
            sums[f] = sums[f] + value * mode
    phase = jnp.concatenate(sums, 0)
    phase = jnp.concatenate([phase * np.float32(1.0 / (1.0 + 0.25 * c)) for c in range(CH)], 0)
    sine, cosine = sin_cos(phase)
    mask = jnp.concatenate([mask_ref[:q]] * FIELDS, 0)
    pupil = jnp.concatenate([mask * cosine, mask * sine], 1)
    half = jnp.concatenate([const_right(pupil, *tables[:2]), const_right(pupil, *tables[2:4])], 1)
    blocks = jnp.concatenate(
        [
            jnp.concatenate(
                [half[f * q : (f + 1) * q, n * SUB : (n + 1) * SUB] for n in (0, 2, 1, 3)], 0
            )
            for f in range(FIELDS)
        ],
        1,
    )
    field = stacked_left(left_twice, left_low, blocks)
    psf = (field[:SUB] * field[:SUB] + field[SUB:] * field[SUB:]) * scale
    return half_plane(psf, rows_twice, rows_low, mixed_high, mixed_low), field, pupil


def backward_math(scale, data, otf, field, pupil, basis_ref, weight_ref, tables):
    mixed_high, mixed_low, rows_high, rows_low, left_high, left_low, right_high, right_low = tables
    weight = weight_ref[PUP // 2 :]
    bars = []
    for c in range(CH):
        parts = []
        cross_real = cross_imag = power = None
        for f in range(c * FRAMES, (c + 1) * FRAMES):
            d, o = data[f * HALF : (f + 1) * HALF], otf[f * HALF : (f + 1) * HALF]
            dr, di, orr, oi = d[:, :SUB], d[:, SUB:], o[:, :SUB], o[:, SUB:]
            parts.append((dr, di, orr, oi))
            terms = (dr * orr + di * oi, di * orr - dr * oi, orr * orr + oi * oi)
            if cross_real is None:
                cross_real, cross_imag, power = terms
            else:
                cross_real = cross_real + terms[0]
                cross_imag = cross_imag + terms[1]
                power = power + terms[2]
        inverse = 1.0 / (power + GAMMA)
        slope = weight * inverse
        xr, xi = cross_real * inverse, cross_imag * inverse
        share = weight * (xr * xr + xi * xi)
        cross_real, cross_imag = cross_real * slope, cross_imag * slope
        for dr, di, orr, oi in parts:
            bar_real = cross_real * dr + cross_imag * di - share * orr
            bar_imag = cross_real * di - cross_imag * dr - share * oi
            bars.append(jnp.concatenate([bar_real, bar_imag], 1))
    columns = const_right(jnp.concatenate(bars, 0), mixed_high, mixed_low)
    stacked = jnp.concatenate(
        [
            jnp.concatenate(
                [columns[f * HALF : (f + 1) * HALF, :SUB], columns[f * HALF : (f + 1) * HALF, SUB:]], 0
            )
            for f in range(FIELDS)
        ],
        1,
    )
    psf_bar = const_left(rows_high, rows_low, stacked) * (2.0 * scale)
    field_bar = jnp.concatenate([field[:SUB] * psf_bar, field[SUB:] * psf_bar], 0)
    half_bar = const_left(left_high, left_low, field_bar)
    q = PUP // 2
    rows = jnp.concatenate(
        [
            jnp.concatenate(
                [half_bar[n * q : (n + 1) * q, f * SUB : (f + 1) * SUB] for n in (0, 2, 1, 3)], 1
            )
            for f in range(FIELDS)
        ],
        0,
    )
    pupil_bar = const_right(rows, right_high, right_low)
    phase_bar = pupil[:, :SUB] * pupil_bar[:, SUB:] - pupil[:, SUB:] * pupil_bar[:, :SUB]
    size = FRAMES * q
    total = phase_bar[:size]
    for c in range(1, CH):
        total = total + phase_bar[c * size : (c + 1) * size] * np.float32(1.0 / (1.0 + 0.25 * c))
    modes = basis_ref.shape[0]
    ones = jnp.ones((8, SUB), F32)
    gap = jnp.zeros((1, SLOT - modes), F32)
    lines = []
    for f in range(FRAMES):
        part = jnp.sum(basis_ref[...] * total[f * q : (f + 1) * q][None], axis=1)
        line = lax.dot_general(
            ones, part, (((1,), (1,)), ((), ())), precision=HIGHEST, preferred_element_type=F32
        )
        lines += [line[:1], gap]
    return jnp.concatenate(
        [jnp.concatenate(lines[:4], 1), jnp.concatenate(lines[4:], 1)], 0
    )


FORWARD = ("right0", "right1", "left", "rows", "mixed")
BACKWARD = ("mixed", "rows_t", "left_t", "right_t")
DATA = ("data_rows", "data_mixed")


def forward_kernel(scale, modes, spots, coeff_ref, basis_ref, fixed_ref, pack_ref, otf_ref, field_ref, pupil_ref):
    tables = views(pack_ref, spots, *FORWARD)
    otf, field, pupil = forward_math(scale, modes, coeff_ref, basis_ref, fixed_ref, tables)
    otf_ref[0] = otf
    field_ref[0] = field
    pupil_ref[0] = pupil


def backward_kernel(
    scale, spots, cells_ref, otf_ref, field_ref, pupil_ref, basis_ref, fixed_ref, pack_ref, data_ref, out_ref
):
    images = jnp.concatenate(
        [cells_ref[:, 0, c, f].reshape(SUB, SUB) for c in range(CH) for f in range(FRAMES)], 1
    )
    data = half_plane(images, *views(pack_ref, spots, *DATA))
    data_ref[0] = data
    tables = views(pack_ref, spots, *BACKWARD)
    out_ref[0] = backward_math(
        scale, data, otf_ref[0], field_ref[0], pupil_ref[0], basis_ref, fixed_ref, tables
    )


def joint_kernel(scale, modes, spots, coeff_ref, data_ref, basis_ref, fixed_ref, pack_ref, out_ref):
    tables = views(pack_ref, spots, *FORWARD)
    otf, field, pupil = forward_math(scale, modes, coeff_ref, basis_ref, fixed_ref, tables)
    tables = views(pack_ref, spots, *BACKWARD)
    out_ref[0] = backward_math(scale, data_ref[0], otf, field, pupil, basis_ref, fixed_ref, tables)


def gather_kernel(n, block_ref, out_ref, send_sem, recv_sem):
    me = lax.axis_index("sub")
    group = n // TR
    start = (me // group) * group
    place = lax.rem(me, group)
    inside = [start + lax.rem(place + step, group) for step in range(1, group)]
    across = [lax.rem(me + step * group, n) for step in range(1, TR)]
    barrier = pltpu.get_barrier_semaphore()
    for peer in inside + across:
        pl.semaphore_signal(barrier, inc=1, device_id=(peer,), device_id_type=pl.DeviceIdType.MESH)
    pl.semaphore_wait(barrier, len(inside) + len(across))

    def copies(source, target, peers, first):
        return [
            pltpu.make_async_remote_copy(
                src_ref=source,
                dst_ref=target,
                send_sem=send_sem.at[first + k],
                recv_sem=recv_sem.at[first + k],
                device_id=(peer,),
                device_id_type=pl.DeviceIdType.MESH,
            )
            for k, peer in enumerate(peers)
        ]

    stage = copies(block_ref, out_ref.at[me], inside, 0)
    for copy in stage:
        copy.start()
    out_ref[me] = block_ref[...]
    for copy in stage:
        copy.wait()
    team = out_ref.at[pl.ds(start, group)]
    stage = copies(team, team, across, len(inside))
    for copy in stage:
        copy.start()
    for copy in stage:
        copy.wait()


def spread_blocks(block, ident):
    n = lax.axis_size("sub")
    return pl.pallas_call(
        functools.partial(gather_kernel, n),
        out_shape=jax.ShapeDtypeStruct((n,) + block.shape, F32),
        in_specs=[pl.BlockSpec(memory_space=pltpu.VMEM)],
        out_specs=pl.BlockSpec(memory_space=pltpu.VMEM),
        scratch_shapes=[pltpu.SemaphoreType.DMA((n,)), pltpu.SemaphoreType.DMA((n,))],
        compiler_params=pltpu.CompilerParams(collective_id=ident, has_side_effects=True),
    )(block)


def whole(array):
    return pl.BlockSpec(array.shape, lambda *_: (0,) * array.ndim, pipeline_mode=pl.Buffered(1))


def on_device(images, anchors, patches, coeffs, zbasis):
    devices = lax.axis_size("sub")
    device = lax.axis_index("sub")
    rows = images.shape[2]
    per = anchors.shape[0]
    owned = coeffs.shape[2]
    modes = coeffs.shape[1]
    tables = make_tables()
    pack, spots = pack_tables(tables)
    pack = jnp.asarray(pack)
    scale = float(1.0 / (SUB * SUB * tables["area"]))

    owned_rows = owned * 2
    tile_rows = -(-(owned_rows + 2) // 8) * 8
    mine = jnp.zeros((tile_rows, SUB), F32)
    packed = coeffs.transpose(2, 0, 1).reshape(owned_rows, 2, modes)
    packed = jnp.pad(packed, ((0, 0), (0, 0), (0, SLOT - modes))).reshape(owned_rows, SUB)
    mine = mine.at[:owned_rows].set(packed)
    owned_row_patch = owned_rows
    mine = mine.at[owned_rows, :per].set(patches.astype(F32))
    mine = mine.at[owned_rows + 1, :per].set(anchors.astype(F32))
    everyone = spread_blocks(mine, 0)
    all_coeffs = everyone[:, :owned_rows, :].reshape(devices * owned, 2 * SUB)
    group = devices // TR
    tile = device // group
    place = device % group
    share = devices * per // TR // group
    all_patches = everyone[:, owned_row_patch, :per].reshape(devices * per // TR, TR)
    all_anchors = everyone[:, owned_row_patch + 1, :per].reshape(devices * per // TR, TR)
    all_patches = all_patches.astype(jnp.int32).T
    pick_tile = (jnp.arange(TR, dtype=jnp.int32) == tile)[None, :]
    tile_anchors = jnp.sum(jnp.where(pick_tile, all_anchors, 0.0), axis=1).astype(jnp.int32)
    patches = lax.dynamic_slice(all_patches, (tile, place * share), (1, share)).reshape(share)
    all_patches = all_patches.reshape(devices * per)

    count = devices * per // TR
    batch = 8
    bands = images.reshape(CH * FRAMES * rows, images.shape[3])
    windows = pl.pallas_call(
        functools.partial(window_kernel, batch),
        grid_spec=pltpu.PrefetchScalarGridSpec(
            num_scalar_prefetch=1,
            grid=(count // batch,),
            in_specs=[pl.BlockSpec(bands.shape, lambda j, a: (0, 0), pipeline_mode=pl.Buffered(1))],
            out_specs=pl.BlockSpec((batch, bands.shape[0], SUB), lambda j, a: (j, 0, 0)),
        ),
        out_shape=jax.ShapeDtypeStruct((count, bands.shape[0], SUB), F32),
        compiler_params=pltpu.CompilerParams(vmem_limit_bytes=VMEM_LIMIT),
    )(tile_anchors, bands)
    teams = [list(range(g * group, (g + 1) * group)) for g in range(TR)]
    received = lax.all_to_all(windows, "sub", 0, 0, axis_index_groups=teams, tiled=True)
    cells = received.reshape(group, share, CH, FRAMES, rows, SUB)
    if rows % 8:
        cells = cells.transpose(1, 2, 3, 0, 4, 5).reshape(1, share, CH, FRAMES, SUB, SUB)
    per = share

    big = pltpu.CompilerParams(vmem_limit_bytes=VMEM_LIMIT)
    basis = zbasis.reshape(modes, PUP // 2, SUB)
    fixed = jnp.asarray(np.concatenate([tables["mask"], tables["weight"]], 0))
    shared = [basis, fixed, pack]
    saved_shapes = [
        jax.ShapeDtypeStruct((per, FIELDS * HALF, 2 * SUB), F32),
        jax.ShapeDtypeStruct((per, 2 * SUB, FIELDS * SUB), F32),
        jax.ShapeDtypeStruct((per, FIELDS * PUP // 2, 2 * SUB), F32),
    ]
    saved_specs = [pl.BlockSpec((1,) + t.shape[1:], lambda s: (s, 0, 0)) for t in saved_shapes]
    slope_shape = jax.ShapeDtypeStruct((per, 2, SUB), F32)
    slope_spec = pl.BlockSpec((1, 2, SUB), lambda s: (s, 0, 0))
    smem = pl.BlockSpec(memory_space=pltpu.SMEM)

    def cost(flops):
        return pl.CostEstimate(flops=flops, bytes_accessed=8 << 20, transcendentals=0)

    def first_slopes(chosen):
        saved = pl.pallas_call(
            functools.partial(forward_kernel, scale, modes, spots),
            grid=(per,),
            in_specs=[smem] + [whole(t) for t in shared],
            out_specs=saved_specs,
            out_shape=saved_shapes,
            compiler_params=big,
            cost_estimate=cost(10**10),
        )(chosen.reshape(per * 2, SUB), *shared)
        cell_spec = pl.BlockSpec(
            (cells.shape[0], 1) + cells.shape[2:], lambda s: (0, s, 0, 0, 0, 0)
        )
        return pl.pallas_call(
            functools.partial(backward_kernel, scale, spots),
            grid=(per,),
            in_specs=[cell_spec]
            + saved_specs
            + [whole(t) for t in shared],
            out_specs=[saved_specs[0], slope_spec],
            out_shape=[saved_shapes[0], slope_shape],
            compiler_params=big,
            cost_estimate=cost(10**10),
        )(cells, *saved, *shared)

    def later_slopes(chosen, data):
        return pl.pallas_call(
            functools.partial(joint_kernel, scale, modes, spots),
            grid=(per,),
            in_specs=[smem, saved_specs[0]] + [whole(t) for t in shared],
            out_specs=slope_spec,
            out_shape=slope_shape,
            compiler_params=big,
            cost_estimate=cost(2 * 10**10),
        )(chosen.reshape(per * 2, SUB), data, *shared)

    patch_ids = jnp.arange(devices * owned, dtype=jnp.int32)
    own_ids = device * owned + jnp.arange(owned, dtype=jnp.int32)
    wanted = jnp.concatenate([patches, own_ids])
    picks = (wanted[:, None] == patch_ids[None, :]).astype(F32)
    current = jnp.dot(picks, all_coeffs, precision=HIGHEST)
    sums = (wanted[:, None] == all_patches[None, :]).astype(F32)
    gradient = jnp.zeros_like(current)
    for iteration in range(ITERS):
        if iteration == 0:
            data, slopes = first_slopes(current[:per])
        else:
            slopes = later_slopes(current[:per], data)
        gathered = spread_blocks(slopes.reshape(per * 2, SUB), 1 + iteration)
        gathered = gathered.reshape(devices * per, 2 * SUB)
        gradient = jnp.dot(sums, gathered, precision=HIGHEST)
        current = current - STEP_SIZE * gradient

    def owned_part(value):
        return value[per:].reshape(owned, FRAMES, SLOT)[:, :, :modes].transpose(1, 2, 0)

    return owned_part(current), owned_part(gradient)


def solution(mesh):
    return jax.shard_map(
        on_device,
        mesh=mesh,
        in_specs=(P(None, None, "sub", None), P("sub"), P("sub"), P(None, None, "sub"), P()),
        out_specs=(P(None, None, "sub"), P(None, None, "sub")),
        check_vma=False,
    )
```
